256 devices in a mesh: expert: 64 (over y, z, core), grid: 4 (over x).
Axes of the slice: x: 4, y: 4, z: 8, core: 2. Of those that a mesh axis runs over, the one named last changes fastest.
Arguments:
- tokens: bfloat16 [32768, 1024], P(('expert', 'grid')), may hold values from -6 to 6
- routes: int32 [32768, 2], P(('expert', 'grid')), may hold values from 0 to 63, all different within a row; in each aligned block of 128 rows (0 to 127, 128 to 255, ...) at most 8 rows name the same one
- route_gates: float32 [32768, 2], P(('expert', 'grid')), may hold values from 0.2 to 1
- caption_lengths: int32 [256, 4], P(('expert', 'grid')), may hold values from 1 to 64, 128 in all within a row
- image_embed: bfloat16 [1024, 1024], P(('expert', 'grid')), may hold values from -6 to 6
- final_gain: float32 [1024], replicated, may hold values from 0.1 to 1.9
- up_weight: bfloat16 [64, 1024, 4096], P('expert', None, 'grid'), may hold values from -0.1875 to 0.1875
- down_weight: bfloat16 [64, 1024, 4096], P('expert', None, 'grid'), may hold values from -0.09375 to 0.09375
Outputs:
- text_embed: float32 [1024, 1024], P(('expert', 'grid'))
- sentence_direction_slope: float32 [1024, 1024], P(('expert', 'grid'))
- picture_direction_slope: float32 [1024, 1024], P(('expert', 'grid'))
The draws below stay inside these ranges and needn't reach their ends.
Inputs may be any that keep to these rules, and one draw needn't show every extreme that they name: `routes`: each token names two different experts; among the 128 tokens of one device no expert is named more than 8 times, and in every draw some device names some expert exactly 8 times. `caption_lengths`: each row gives the token counts of one device's 4 captions, summing to 128; the largest of a row is exactly 64.
All inputs are finite; a program needn't handle non-finite values.
Results may differ from the reference program's by a relative error of at most 0.003.
Values may be sent and summed in bfloat16 or wider, within the bound.
No kernel may reach another device: no remote copies, remote signals or barrier semaphores. Data moves between devices by JAX's collectives and lax.ppermute only.
A program may use at most 64 MiB of HBM per device.

```python
import math
import jax
import jax.numpy as jnp
import numpy as np
from jax import lax

D = 1024
FF = 4096
TOK_DEV = 128
CAPT_DEV = 4
EXPERTS = 64
CAP = 8
TOKENS = 32768
CAPTIONS = 1024
N_EXPERT = 64
N_GRID = 4


def shared_directions(key, owners):
    common = jax.random.normal(jax.random.fold_in(key, 101), (D,), jnp.float32)
    paired = jax.random.normal(jax.random.fold_in(key, 202), (owners, D), jnp.float32)
    owner_signs = jnp.where(jax.random.bernoulli(jax.random.fold_in(key, 303), 0.5, (owners,)), 1.0, -1.0).astype(jnp.float32)
    return (common, paired, owner_signs)


def draw_tokens(key, part):
    owners = TOKENS // TOK_DEV
    common, paired, owner_signs = shared_directions(key, owners)
    noise_key = jax.random.fold_in(key, 11)
    noise = jax.random.normal(noise_key, (owners, TOK_DEV, D), jnp.float32)
    common_amount = 0.1
    paired_amount = 0.2
    values = noise + common_amount * owner_signs[:, None, None] * common[None, None, :] + paired_amount * paired[:, None, :]
    return jnp.clip(values.reshape(TOKENS, D), -6.0, 6.0).astype(jnp.bfloat16)


def draw_image_embed(key, part):
    owners = TOKENS // TOK_DEV
    common, paired, owner_signs = shared_directions(key, owners)
    noise_key = jax.random.fold_in(key, 22)
    row_signs = jnp.where(jax.random.bernoulli(jax.random.fold_in(key, 404), 0.5, (CAPTIONS,)), 1.0, -1.0).astype(jnp.float32)
    noise = jax.random.normal(noise_key, (CAPTIONS, D), jnp.float32)
    strength = jax.random.uniform(jax.random.fold_in(key, 505), (CAPTIONS,), jnp.float32, 0.5, 1.5)
    common_amount = 0.3
    owner_rows = jnp.repeat(paired, CAPT_DEV, axis=0)
    values = noise + common_amount * row_signs[:, None] * common[None, :] + strength[:, None] * owner_rows
    return jnp.clip(values, -6.0, 6.0).astype(jnp.bfloat16)


def block_levels(stream_key, dims, shards, low, top_value):
    gain = 1.0
    for axis_at, shards_of in shards:
        draws = jax.random.uniform(jax.random.fold_in(jax.random.fold_in(stream_key, 6), axis_at), (shards_of,), jnp.float32, low / len(shards), top_value / len(shards))
        gain = gain * jnp.repeat(jnp.exp(draws), dims[axis_at] // shards_of).reshape((-1,) + (1,) * (len(dims) - 1 - axis_at))
    return gain


def split_up(count, total, most, skew):
    weights = [(1 << 20) // math.isqrt(standing ** skew) + 1 for standing in range(2, count + 1)]
    rest, holding = total - most - (count - 1), [1] * (count - 1)
    while rest > 0:
        candidates = [i for i in range(count - 1) if holding[i] < most]
        whole, left = sum([weights[i] for i in candidates]), rest
        for i in candidates:
            extra = min(most - holding[i], max(1, left * weights[i] // whole), rest)
            holding[i] = holding[i] + extra
            rest = rest - extra
    return np.array([most] + holding)


def uneven(key, count, total, most, skew):
    if count == 2:
        one = jax.random.randint(key, (), max(1, total - most), min(most, total - 1) + 1)
        return jnp.stack([one, total - one])
    lengths = jnp.asarray(split_up(count, total, most, skew), jnp.int32)
    twos = (count - 1) // 2
    giver, sink = lengths[1:1 + 2 * twos:2], lengths[2:2 + 2 * twos:2]
    margin = jnp.minimum(giver - 1, most - sink)
    moved = jax.random.randint(jax.random.fold_in(key, 1), (twos,), 0, 1 << 20) % (margin + 1)
    lengths = lengths.at[1:1 + 2 * twos:2].set(giver - moved).at[2:2 + 2 * twos:2].set(sink + moved)
    return lengths[jax.random.permutation(jax.random.fold_in(key, 2), count)]


def shared_out(own_key, own, number, rows, number_of, top, most, lean):
    order = jax.random.permutation(own_key, number_of)
    heavy_load, ordinary = shares(number_of, rows * top, most, lean, True), shares(number_of, rows * top, most, lean, False)
    places = jnp.arange(number_of)

    def named(sizes, turn):
        used = int((sizes > 0).sum())
        fixed = max(1, used // 4)
        moved = fixed + (places - fixed + turn * (used - fixed)) % max(1, number_of - fixed)
        return jnp.zeros((number_of,), jnp.int32).at[order[jnp.where(places < fixed, places, moved)]].set(jnp.asarray(sizes, jnp.int32))

    sizes = jnp.where(number % 4 == 0, named(heavy_load, number // 4), named(ordinary, number - number // 4 - 1))
    mixed = jax.random.permutation(jax.random.fold_in(own, 3), number_of)
    source_of, sink = mixed[0:number_of // 2 * 2:2], mixed[1:number_of // 2 * 2:2]
    margin = jnp.minimum(sizes[source_of] - 1, most - sizes[sink]) // 2
    margin = jnp.where((source_of == order[0]) | (sink == order[0]) | (sizes[sink] == 0), 0, jnp.maximum(margin, 0))
    moved = jax.random.randint(jax.random.fold_in(own, 4), (number_of // 2,), 0, 1 << 20) % (margin + 1)
    sizes = sizes.at[source_of].add(-moved).at[sink].add(moved)
    items = jnp.searchsorted(jnp.cumsum(sizes), jnp.arange(rows * top), side="right").astype(jnp.int32)
    table = items.reshape(top, rows).T
    table = table[jax.random.permutation(jax.random.fold_in(own, 1), rows)]
    turn = jax.random.randint(jax.random.fold_in(own, 2), (rows, 1), 0, top)
    return jnp.take_along_axis(table, (jnp.arange(top)[None, :] + turn) % top, axis=1)


def shares(number_of, total, most, slope, full):
    portions = [(1 << 20) // math.isqrt(grade ** slope) + 1 for grade in range(1, number_of + 1)]
    largest = most if full else min(most, max(-(-total // number_of), total * portions[0] // sum(portions)))
    least = 1 if total - largest >= number_of - 1 else 0
    given, spare = [largest] + [least] * (number_of - 1), total - largest - least * (number_of - 1)
    while spare > 0:
        movable = [i for i in range(1, number_of) if given[i] < largest] or [i for i in range(1, number_of) if given[i] < most]
        mass, left = sum([portions[i] for i in movable]), spare
        for i in movable:
            extra = min(most - given[i], max(1, left * portions[i] // mass), spare)
            given[i] = given[i] + extra
            spare = spare - extra
    return np.array(given)


def normal_values(rng, extent, width, most, split=(), held_as=jnp.bfloat16):
    entries = jax.random.normal(rng, extent, jnp.float32) * width
    if len(split) > 0:
        entries = block_levels(rng, extent, split, -0.22, 0.18) * entries
    return jnp.clip(entries, min=-most, max=most).astype(held_as)


def setup_inputs(seed: int = 0) -> dict:
    keys = jax.random.split(jax.random.key(seed), 9)
    tokens = draw_tokens(jax.random.fold_in(keys[8], 71), 0)
    routes_keys = jax.random.split(jax.random.fold_in(keys[1], 1), TOKENS // TOK_DEV)
    routes_turns = jax.random.permutation(jax.random.fold_in(keys[1], 3), TOKENS // TOK_DEV)
    routes = jax.vmap(lambda own, number: shared_out(jax.random.fold_in(keys[1], 2), own, number, TOK_DEV, EXPERTS, 2, CAP, 2))(routes_keys, routes_turns).reshape((TOKENS, 2))
    route_gates = jnp.clip(0.2 + 0.8 * jax.random.uniform(keys[2], (TOKENS, 2), jnp.float32) ** block_levels(keys[2], (TOKENS, 2), ((0, 256),), -0.2, 0.2), 0.2, 1.0)
    caption_lengths = jax.vmap(lambda own: uneven(own, CAPT_DEV, TOK_DEV, TOK_DEV // 2, 1))(jax.random.split(keys[3], (N_EXPERT * N_GRID))).reshape((N_EXPERT * N_GRID, CAPT_DEV)).astype(jnp.int32)
    image_embed = draw_image_embed(jax.random.fold_in(keys[8], 71), 0)
    final_gain = jnp.clip(1.0 + 0.18 * jax.random.normal(keys[5], (D,), jnp.float32), 0.1, 1.9)
    up_weight = normal_values(keys[6], (EXPERTS, D, FF), D ** -0.5, 0.1875, ((0, 64), (2, 4)))
    down_weight = normal_values(keys[7], (EXPERTS, D, FF), FF ** -0.5, 0.09375, ((0, 64), (2, 4)))
    return dict(tokens=tokens, routes=routes, route_gates=route_gates, caption_lengths=caption_lengths, image_embed=image_embed, final_gain=final_gain, up_weight=up_weight, down_weight=down_weight)


EPSILON = 1e-06
SIMILARITY_HEAT = 10.0

def layer_norm(values):
    centred = values - lax.optimization_barrier(jnp.mean(values, axis=-1, keepdims=True))
    return centred * lax.rsqrt(lax.optimization_barrier(jnp.mean(centred * centred, axis=-1, keepdims=True)) + EPSILON)

def reference(tokens, routes, route_gates, caption_lengths, image_embed, final_gain, up_weight, down_weight):
    devices = N_EXPERT * N_GRID
    stream = tokens.astype(jnp.float32).reshape(devices, TOK_DEV, D)
    normed = layer_norm(stream).astype(jnp.bfloat16)
    chosen = routes.reshape(devices, 2 * TOK_DEV)
    expert_hot = (chosen[:, :, None] == jnp.arange(EXPERTS, dtype=jnp.int32)[None, None, :]).astype(jnp.int32)
    before = jnp.cumsum(expert_hot, axis=1) - expert_hot
    slot_of = lax.optimization_barrier(jnp.sum(before * expert_hot, axis=2)).astype(jnp.int32)
    position = (chosen * CAP + slot_of).astype(jnp.int32)

    def build(inputs):
        rows, places = inputs
        repeated = jnp.repeat(rows, 2, axis=0)
        return jnp.zeros((EXPERTS * CAP, D), jnp.bfloat16).at[places].set(repeated)
    buffers = lax.map(build, (normed, position))
    per_expert = buffers.reshape(devices, EXPERTS, CAP, D).transpose(1, 0, 2, 3).reshape(EXPERTS, devices * CAP, D)
    quarter = FF // N_GRID

    def run_expert(inputs):
        rows, up_matrix, down_matrix = inputs
        total = jnp.zeros((rows.shape[0], D), jnp.float32)
        for index in range(N_GRID):
            low = index * quarter
            hidden = jax.nn.gelu(jnp.dot(rows, up_matrix[:, low:low + quarter], preferred_element_type=jnp.float32), approximate=False).astype(jnp.bfloat16)
            term = jnp.dot(hidden, down_matrix[:, low:low + quarter].T, preferred_element_type=jnp.float32)
            total = total + lax.optimization_barrier(term.astype(jnp.bfloat16)).astype(jnp.float32)
        return total.astype(jnp.bfloat16)
    outputs = lax.map(run_expert, (per_expert, up_weight, down_weight))
    back = outputs.reshape(EXPERTS, devices, CAP, D).transpose(1, 0, 2, 3).reshape(devices, EXPERTS * CAP, D)
    picked = jax.vmap(lambda table, places: table[places])(back, position).astype(jnp.float32)
    weighted = picked * route_gates.reshape(devices, 2 * TOK_DEV)[:, :, None]
    mixed = stream + lax.optimization_barrier(jnp.sum(weighted.reshape(devices, TOK_DEV, 2, D), axis=2))
    final = layer_norm(mixed) * final_gain
    ends = jnp.cumsum(caption_lengths, axis=1)
    starts = ends - caption_lengths
    spots = jnp.arange(TOK_DEV, dtype=jnp.int32)
    members = ((spots[None, None, :] >= starts[:, :, None]) & (spots[None, None, :] < ends[:, :, None])).astype(jnp.float32)
    pooled = jnp.einsum('sct,std->scd', members, final, precision=lax.Precision.HIGHEST)
    pooled = pooled / caption_lengths[:, :, None].astype(jnp.float32)
    pooled = pooled.reshape(CAPTIONS, D)
    text_embed = pooled * lax.rsqrt(lax.optimization_barrier(jnp.mean(pooled * pooled, axis=-1, keepdims=True)) + EPSILON)
    root = jnp.sqrt(jnp.float32(D))
    sentence_average = (text_embed / root).astype(jnp.bfloat16)
    sentence_direction = sentence_average.astype(jnp.float32)
    image_values = image_embed.astype(jnp.float32)
    picture_average = (image_values * lax.rsqrt(lax.optimization_barrier(jnp.mean(image_values * image_values, axis=-1, keepdims=True)) + EPSILON) / root).astype(jnp.bfloat16)
    picture_direction = picture_average.astype(jnp.float32)
    match_similarity_matrix = SIMILARITY_HEAT * jnp.dot(picture_average, sentence_average.T, preferred_element_type=jnp.float32)
    labels = jnp.arange(CAPTIONS, dtype=jnp.int32)
    signs = jnp.where(labels[:, None] == labels[None, :], 1.0, -1.0).astype(jnp.float32)
    objective_multiplier = -signs * jax.nn.sigmoid(-signs * match_similarity_matrix)
    picture_direction_slope = SIMILARITY_HEAT * jnp.dot(objective_multiplier, sentence_direction, precision=lax.Precision.HIGHEST)
    sentence_direction_slope = SIMILARITY_HEAT * jnp.dot(objective_multiplier.T, picture_direction, precision=lax.Precision.HIGHEST)
    return (text_embed, sentence_direction_slope, picture_direction_slope)
```

```python
import math

import jax
import jax.numpy as jnp
from jax import lax
from jax.sharding import PartitionSpec as P

EPSILON = 1e-06
SIMILARITY_HEAT = 10.0
BF16 = jnp.bfloat16
F32 = jnp.float32


def layer_norm(values):
    centred = values - jnp.mean(values, axis=-1, keepdims=True)
    return centred * lax.rsqrt(jnp.mean(centred * centred, axis=-1, keepdims=True) + EPSILON)


def expert_part(rows, up_piece, down_piece):
    hidden = jax.nn.gelu(
        jnp.dot(rows, up_piece, preferred_element_type=F32), approximate=False
    ).astype(BF16)
    return lax.dot_general(
        hidden, down_piece, (((1,), (1,)), ((), ())), preferred_element_type=F32
    ).astype(BF16)


def split_pair(values):
    high = values.astype(BF16)
    return high, (values - high.astype(F32)).astype(BF16)


def pair_slope(logits, same):
    signs = jnp.where(same, 1.0, -1.0).astype(F32)
    return -signs * jax.nn.sigmoid(-signs * logits)


def weighted_sum(coeff, rows):
    high, low = split_pair(coeff)
    both = jnp.dot(jnp.concatenate([high, low], axis=0), rows, preferred_element_type=F32)
    count = coeff.shape[0]
    return SIMILARITY_HEAT * (both[:count] + both[count:])


def ring_shift(values, step, size):
    return lax.ppermute(values, "grid", [(i, (i + step) % size) for i in range(size)])


def unit_rows(values):
    return values * lax.rsqrt(jnp.mean(values * values, axis=-1, keepdims=True) + EPSILON)


def on_device(
    tokens, routes, route_gates, caption_lengths, image_embed, final_gain, up_weight, down_weight
):
    token_count, width = tokens.shape
    experts_all = lax.axis_size("expert")
    grid_all = lax.axis_size("grid")
    slots = 4 * token_count // experts_all
    places_all = experts_all * slots
    scale_root = math.sqrt(width)
    expert_id = lax.axis_index("expert")

    picture_unit = (unit_rows(image_embed.astype(F32)) / scale_root).astype(BF16)
    captions_here = picture_unit.shape[0]
    pictures_all = lax.all_gather(picture_unit, ("expert", "grid"), axis=0, tiled=True)
    pictures_row = jnp.concatenate(
        [picture_unit] + [ring_shift(picture_unit, k, grid_all) for k in range(1, grid_all)], axis=0
    )

    stream = tokens.astype(F32)
    normed = layer_norm(stream).astype(BF16)
    first, second = routes[:, 0:1], routes[:, 1:2]
    names = jnp.arange(experts_all, dtype=jnp.int32)[None, :]
    hot_first = first == names
    hot_second = second == names
    both_hot = jnp.concatenate([hot_first, hot_second], axis=1).astype(BF16)
    order = jnp.arange(token_count, dtype=jnp.int32)
    before = (order[None, :] < order[:, None]).astype(BF16)
    ranks = jnp.dot(before, both_hot, preferred_element_type=F32)
    totals = jnp.sum(hot_first.astype(F32), axis=0, keepdims=True)
    rank_first = jnp.sum(jnp.where(hot_first, ranks[:, :experts_all], 0.0), axis=1, keepdims=True)
    rank_second = jnp.sum(
        jnp.where(hot_second, ranks[:, experts_all:] + totals, 0.0), axis=1, keepdims=True
    )
    place_first = first * slots + rank_first.astype(jnp.int32)
    place_second = second * slots + rank_second.astype(jnp.int32)
    spots = jnp.arange(places_all, dtype=jnp.int32)[None, :]
    at_first = spots == place_first
    at_second = spots == place_second
    chosen = (at_first | at_second).astype(BF16)
    send = lax.dot_general(chosen, normed, (((0,), (0,)), ((), ())), preferred_element_type=F32)
    send = send.astype(BF16).reshape(experts_all, slots, width)
    arrived = lax.all_to_all(send, "expert", split_axis=0, concat_axis=0, tiled=True)
    rows = arrived.reshape(places_all, width)

    up_local = up_weight[0]
    down_local = down_weight[0]
    pieces = [rows] + [ring_shift(rows, k, grid_all) for k in range(1, grid_all)]
    total = expert_part(pieces[0], up_local, down_local).astype(F32)
    for k in (1, 3, 2):
        term = expert_part(pieces[k], up_local, down_local)
        total = total + ring_shift(term, -k, grid_all).astype(F32)
    results = total.astype(BF16).reshape(experts_all, slots, width)
    returned = lax.all_to_all(results, "expert", split_axis=0, concat_axis=0, tiled=True)
    returned = returned.reshape(places_all, width)

    gates = jnp.where(at_first, route_gates[:, 0:1], 0.0) + jnp.where(
        at_second, route_gates[:, 1:2], 0.0
    )
    gate_high, gate_low = split_pair(gates)
    mixed = (
        stream
        + jnp.dot(gate_high, returned, preferred_element_type=F32)
        + jnp.dot(gate_low, returned, preferred_element_type=F32)
    )
    final = layer_norm(mixed) * final_gain
    lengths = caption_lengths[0]
    ends = jnp.cumsum(lengths)
    starts = ends - lengths
    members = ((order[None, :] >= starts[:, None]) & (order[None, :] < ends[:, None])).astype(F32)
    pooled = jnp.dot(members, final, precision=lax.Precision.HIGHEST) / lengths[:, None].astype(F32)
    text_embed = unit_rows(pooled)
    text_unit = (text_embed / scale_root).astype(BF16)

    spread = jnp.broadcast_to(text_unit[None], (experts_all,) + text_unit.shape)
    text_column = lax.all_to_all(spread, "expert", split_axis=0, concat_axis=0, tiled=True)
    text_column = text_column.reshape(-1, width)
    logits = SIMILARITY_HEAT * lax.dot_general(
        pictures_row, text_column, (((1,), (1,)), ((), ())), preferred_element_type=F32
    )
    row_ids = jnp.arange(pictures_row.shape[0], dtype=jnp.int32)[:, None]
    column_ids = jnp.arange(text_column.shape[0], dtype=jnp.int32)[None, :]
    same = (row_ids < captions_here) & (row_ids + expert_id * captions_here == column_ids)
    coeff = pair_slope(logits, same)
    partial = weighted_sum(coeff, text_column).reshape(grid_all, captions_here, width)
    picture_slope = partial[0]
    for k in range(1, grid_all):
        picture_slope = picture_slope + ring_shift(partial[k], -k, grid_all)

    mine = (expert_id * grid_all + lax.axis_index("grid")) * captions_here
    own_logits = SIMILARITY_HEAT * lax.dot_general(
        text_unit, pictures_all, (((1,), (1,)), ((), ())), preferred_element_type=F32
    )
    own_ids = mine + jnp.arange(captions_here, dtype=jnp.int32)[:, None]
    every = jnp.arange(pictures_all.shape[0], dtype=jnp.int32)[None, :]
    own_coeff = pair_slope(own_logits, own_ids == every)
    sentence_slope = weighted_sum(own_coeff, pictures_all)
    return (text_embed, sentence_slope, picture_slope)


def solution(mesh):
    split = P(("expert", "grid"), None)
    weights = P("expert", None, "grid")
    return jax.shard_map(
        on_device,
        mesh=mesh,
        in_specs=(split, split, split, split, split, P(), weights, weights),
        out_specs=(split, split, split),
        check_vma=False,
    )
```

```python
import math

import jax
import jax.numpy as jnp
from jax import lax
from jax.experimental import pallas as pl
from jax.experimental.pallas import tpu as pltpu
from jax.sharding import PartitionSpec as P

EPSILON = 1e-06
SIMILARITY_HEAT = 10.0
BF16 = jnp.bfloat16
F32 = jnp.float32


def layer_norm(values):
    centred = values - jnp.mean(values, axis=-1, keepdims=True)
    return centred * lax.rsqrt(jnp.mean(centred * centred, axis=-1, keepdims=True) + EPSILON)


def expert_kernel(rows_ref, up_ref, down_ref, out_ref, total_ref):
    step = pl.program_id(0)
    hidden = jnp.dot(rows_ref[...], up_ref[...], preferred_element_type=F32)
    hidden = (0.5 * hidden * (1.0 + lax.erf(hidden * math.sqrt(0.5)))).astype(BF16)
    term = lax.dot_general(
        hidden, down_ref[...], (((1,), (1,)), ((), ())), preferred_element_type=F32
    )

    @pl.when(step == 0)
    def _():
        total_ref[...] = term

    @pl.when(step > 0)
    def _():
        total_ref[...] += term

    @pl.when(step == pl.num_programs(0) - 1)
    def _():
        out_ref[...] = total_ref[...].astype(BF16)


def expert_part(rows, up_piece, down_piece):
    count, width = rows.shape
    units = up_piece.shape[1]
    tile = min(256, units)
    return pl.pallas_call(
        expert_kernel,
        grid=(units // tile,),
        in_specs=[
            pl.BlockSpec((count, width), lambda i: (0, 0)),
            pl.BlockSpec((width, tile), lambda i: (0, i)),
            pl.BlockSpec((width, tile), lambda i: (0, i)),
        ],
        out_specs=pl.BlockSpec((count, width), lambda i: (0, 0)),
        out_shape=jax.ShapeDtypeStruct((count, width), BF16),
        scratch_shapes=[pltpu.VMEM((count, width), F32)],
        compiler_params=pltpu.CompilerParams(vmem_limit_bytes=24 * 2**20),
        cost_estimate=pl.CostEstimate(
            flops=16 * count * width * units,
            bytes_accessed=4 * width * units + 4 * count * width,
            transcendentals=count * units,
        ),
    )(rows, up_piece, down_piece)


def split_pair(values):
    high = values.astype(BF16)
    return high, (values - high.astype(F32)).astype(BF16)


def pair_slope(logits, same):
    signs = jnp.where(same, 1.0, -1.0).astype(F32)
    return -signs * jax.nn.sigmoid(-signs * logits)


def weighted_sum(coeff, rows):
    high, low = split_pair(coeff)
    both = jnp.dot(jnp.concatenate([high, low], axis=0), rows, preferred_element_type=F32)
    count = coeff.shape[0]
    return SIMILARITY_HEAT * (both[:count] + both[count:])


def held(*values):
    return lax.optimization_barrier(values)


def moved(values, target, mesh_shape):
    wide, deep, cores = mesh_shape
    pairs = []
    for index in range(wide * deep * cores):
        y, z, core = index // (deep * cores), index // cores % deep, index % cores
        y, z, core = target(y, z, core)
        pairs.append((index, (y % wide * deep + z % deep) * cores + core % cores))
    return lax.ppermute(values, "expert", pairs)


def along_y(mine, shape):
    others = [moved(mine, lambda y, z, c, k=k: (y + k, z, c), shape) for k in range(1, shape[0])]
    return jnp.concatenate([mine] + others, axis=0)


def along_z(group, shape):
    deep = shape[1]
    both = jnp.concatenate([group, moved(group, lambda y, z, c: (y, z, c + 1), shape)], axis=0)
    here = [
        moved(both, lambda y, z, c, k=k: (y, z + (k if c == 0 else -k), c), shape)
        for k in range(1, deep // 2)
    ]
    here.append(moved(group, lambda y, z, c: (y, z + deep // 2, c), shape))
    return both, jnp.concatenate(here, axis=0)


def last_swap(both, here, shape):
    other = moved(here, lambda y, z, c: (y, z, c + 1), shape)
    return jnp.concatenate([both, here, other], axis=0)


def ring_shift(values, step, size):
    return lax.ppermute(values, "grid", [(i, (i + step) % size) for i in range(size)])


def unit_rows(values):
    return values * lax.rsqrt(jnp.mean(values * values, axis=-1, keepdims=True) + EPSILON)


def on_device(
    tokens, routes, route_gates, caption_lengths, image_embed, final_gain, up_weight, down_weight
):
    token_count, width = tokens.shape
    experts_all = lax.axis_size("expert")
    grid_all = lax.axis_size("grid")
    slots = 4 * token_count // experts_all
    places_all = experts_all * slots
    scale_root = math.sqrt(width)

    picture_unit = (unit_rows(image_embed.astype(F32)) / scale_root).astype(BF16)
    captions_here = picture_unit.shape[0]
    shape = (grid_all, experts_all // (2 * grid_all), 2)
    row_parts = [picture_unit] + [ring_shift(picture_unit, k, grid_all) for k in range(1, grid_all)]
    picture_group = along_y(picture_unit, shape)

    stream = tokens.astype(F32)
    normed = layer_norm(stream).astype(BF16)
    first, second = routes[:, 0:1], routes[:, 1:2]
    names = jnp.arange(experts_all, dtype=jnp.int32)[None, :]
    hot_first = first == names
    hot_second = second == names
    both_hot = jnp.concatenate([hot_first, hot_second], axis=1).astype(BF16)
    order = jnp.arange(token_count, dtype=jnp.int32)
    before = (order[None, :] < order[:, None]).astype(BF16)
    ranks = jnp.dot(before, both_hot, preferred_element_type=F32)
    totals = jnp.sum(hot_first.astype(F32), axis=0, keepdims=True)
    rank_first = jnp.sum(jnp.where(hot_first, ranks[:, :experts_all], 0.0), axis=1, keepdims=True)
    rank_second = jnp.sum(
        jnp.where(hot_second, ranks[:, experts_all:] + totals, 0.0), axis=1, keepdims=True
    )
    half = slots // 2
    rank_first, rank_second = rank_first.astype(jnp.int32), rank_second.astype(jnp.int32)
    place_first = (rank_first // half * experts_all + first) * half + rank_first % half
    place_second = (rank_second // half * experts_all + second) * half + rank_second % half
    spots = jnp.arange(places_all, dtype=jnp.int32)[None, :]
    at_first = spots == place_first
    at_second = spots == place_second
    chosen = (at_first | at_second).astype(BF16)
    send = lax.dot_general(chosen, normed, (((0,), (0,)), ((), ())), preferred_element_type=F32)
    send = send.astype(BF16).reshape(2, experts_all, half, width)

    up_local = up_weight[0]
    down_local = down_weight[0]
    half_places = experts_all * half
    arrived = lax.all_to_all(send[0], "expert", split_axis=0, concat_axis=0, tiled=True)
    arrived, send_late, picture_group, *row_parts = held(
        arrived, send[1], picture_group, *row_parts
    )
    pictures_row = jnp.concatenate(row_parts, axis=0)
    early = arrived.reshape(half_places, width)
    early_pieces = [early] + [ring_shift(early, k, grid_all) for k in range(1, grid_all)]
    picture_both, picture_here = along_z(picture_group, shape)
    arrived = lax.all_to_all(send_late, "expert", split_axis=0, concat_axis=0, tiled=True)
    arrived, picture_both, picture_here = held(arrived, picture_both, picture_here)
    late = arrived.reshape(half_places, width)
    late_pieces = [late] + [ring_shift(late, k, grid_all) for k in range(1, grid_all)]

    early_terms = [expert_part(piece, up_local, down_local) for piece in early_pieces]
    early_back = [early_terms[0]] + [
        ring_shift(early_terms[k], -k, grid_all) for k in range(1, grid_all)
    ]
    late_terms = [expert_part(piece, up_local, down_local) for piece in late_pieces]
    late_back = [late_terms[0]] + [
        ring_shift(late_terms[k], -k, grid_all) for k in range(1, grid_all)
    ]
    early_sum = sum(term.astype(F32) for term in early_back).astype(BF16)
    early_home = lax.all_to_all(
        early_sum.reshape(experts_all, half, width), "expert", split_axis=0, concat_axis=0, tiled=True
    )
    pictures_column = last_swap(picture_both, picture_here, shape)
    late_sum = sum(term.astype(F32) for term in late_back).astype(BF16)
    late_sum, pictures_column = held(late_sum, pictures_column)
    late_home = lax.all_to_all(
        late_sum.reshape(experts_all, half, width), "expert", split_axis=0, concat_axis=0, tiled=True
    )
    returned = jnp.concatenate(
        [early_home.reshape(half_places, width), late_home.reshape(half_places, width)], axis=0
    )

    gates = jnp.where(at_first, route_gates[:, 0:1], 0.0) + jnp.where(
        at_second, route_gates[:, 1:2], 0.0
    )
    gate_high, gate_low = split_pair(gates)
    mixed = (
        stream
        + jnp.dot(gate_high, returned, preferred_element_type=F32)
        + jnp.dot(gate_low, returned, preferred_element_type=F32)
    )
    final = layer_norm(mixed) * final_gain
    lengths = caption_lengths[0]
    ends = jnp.cumsum(lengths)
    starts = ends - lengths
    members = ((order[None, :] >= starts[:, None]) & (order[None, :] < ends[:, None])).astype(F32)
    pooled = jnp.dot(members, final, precision=lax.Precision.HIGHEST) / lengths[:, None].astype(F32)
    text_embed = unit_rows(pooled)
    text_unit = (text_embed / scale_root).astype(BF16)

    text_parts = [text_unit] + [ring_shift(text_unit, k, grid_all) for k in range(1, grid_all)]
    text_group = along_y(text_unit, shape)
    text_both, text_here = along_z(text_group, shape)
    text_column = last_swap(text_both, text_here, shape)
    text_row = jnp.concatenate(text_parts, axis=0)

    def slopes(mine, others):
        logits = SIMILARITY_HEAT * lax.dot_general(
            mine, others, (((1,), (1,)), ((), ())), preferred_element_type=F32
        )
        row_ids = lax.broadcasted_iota(jnp.int32, logits.shape, 0)
        column_ids = lax.broadcasted_iota(jnp.int32, logits.shape, 1)
        same = (row_ids < captions_here) & (row_ids == column_ids)
        return weighted_sum(pair_slope(logits, same), others)

    partial = jnp.concatenate(
        [
            slopes(text_row, pictures_column).reshape(grid_all, captions_here, width),
            slopes(pictures_row, text_column).reshape(grid_all, captions_here, width),
        ],
        axis=1,
    )
    slope = partial[0]
    for k in range(1, grid_all):
        slope = slope + ring_shift(partial[k], -k, grid_all)
    return (text_embed, slope[:captions_here], slope[captions_here:])


def solution(mesh):
    split = P(("expert", "grid"), None)
    weights = P("expert", None, "grid")
    return jax.shard_map(
        on_device,
        mesh=mesh,
        in_specs=(split, split, split, split, split, P(), weights, weights),
        out_specs=(split, split, split),
        check_vma=False,
    )
```

```python
import math

import jax
import jax.numpy as jnp
from jax import lax
from jax.experimental import pallas as pl
from jax.experimental.pallas import tpu as pltpu
from jax.sharding import PartitionSpec as P

EPSILON = 1e-06
SIMILARITY_HEAT = 10.0
BF16 = jnp.bfloat16
F32 = jnp.float32


def layer_norm(values):
    centred = values - jnp.mean(values, axis=-1, keepdims=True)
    return centred * lax.rsqrt(jnp.mean(centred * centred, axis=-1, keepdims=True) + EPSILON)


def expert_kernel(rows_ref, up_ref, down_ref, out_ref, total_ref):
    step = pl.program_id(0)
    hidden = jnp.dot(rows_ref[...], up_ref[...], preferred_element_type=F32)
    hidden = (0.5 * hidden * (1.0 + lax.erf(hidden * math.sqrt(0.5)))).astype(BF16)
    term = lax.dot_general(
        hidden, down_ref[...], (((1,), (1,)), ((), ())), preferred_element_type=F32
    )

    @pl.when(step == 0)
    def _():
        total_ref[...] = term

    @pl.when(step > 0)
    def _():
        total_ref[...] += term

    @pl.when(step == pl.num_programs(0) - 1)
    def _():
        out_ref[...] = total_ref[...].astype(BF16)


def expert_part(rows, up_piece, down_piece):
    count, width = rows.shape
    units = up_piece.shape[1]
    tile = min(256, units)
    return pl.pallas_call(
        expert_kernel,
        grid=(units // tile,),
        in_specs=[
            pl.BlockSpec((count, width), lambda i: (0, 0)),
            pl.BlockSpec((width, tile), lambda i: (0, i)),
            pl.BlockSpec((width, tile), lambda i: (0, i)),
        ],
        out_specs=pl.BlockSpec((count, width), lambda i: (0, 0)),
        out_shape=jax.ShapeDtypeStruct((count, width), BF16),
        scratch_shapes=[pltpu.VMEM((count, width), F32)],
        compiler_params=pltpu.CompilerParams(vmem_limit_bytes=56 * 2**20),
        cost_estimate=pl.CostEstimate(
            flops=16 * count * width * units,
            bytes_accessed=4 * width * units + 4 * count * width,
            transcendentals=count * units,
        ),
    )(rows, up_piece, down_piece)


def split_pair(values):
    high = values.astype(BF16)
    return high, (values - high.astype(F32)).astype(BF16)


def pair_slope(logits, same):
    signs = jnp.where(same, 1.0, -1.0).astype(F32)
    return -signs * jax.nn.sigmoid(-signs * logits)


def weighted_sum(coeff, rows):
    high, low = split_pair(coeff)
    both = jnp.dot(jnp.concatenate([high, low], axis=0), rows, preferred_element_type=F32)
    count = coeff.shape[0]
    return SIMILARITY_HEAT * (both[:count] + both[count:])


def held(*values):
    return lax.optimization_barrier(values)


def moved(values, target, mesh_shape):
    wide, deep, cores = mesh_shape
    pairs = []
    for index in range(wide * deep * cores):
        y, z, core = index // (deep * cores), index // cores % deep, index % cores
        y, z, core = target(y, z, core)
        pairs.append((index, (y % wide * deep + z % deep) * cores + core % cores))
    return lax.ppermute(values, "expert", pairs)


def along_y(mine, shape):
    others = [moved(mine, lambda y, z, c, k=k: (y + k, z, c), shape) for k in range(1, shape[0])]
    return jnp.concatenate([mine] + others, axis=0)


def along_expert(mine, shape):
    wide, deep, cores = shape
    chips = wide * deep
    groups = [[chip * cores + core for chip in range(chips)] for core in range(cores)]
    copies = jnp.broadcast_to(mine[None], (chips,) + mine.shape)
    column = lax.all_to_all(
        copies, "expert", split_axis=0, concat_axis=0, axis_index_groups=groups, tiled=True
    ).reshape(chips * mine.shape[0], mine.shape[1])
    return on_chip(column, shape)


def on_chip(group, shape):
    return jnp.concatenate([group, moved(group, lambda y, z, c: (y, z, c + 1), shape)], axis=0)


def along_z(group, both, shape):
    deep = shape[1]
    here = [
        moved(both, lambda y, z, c, k=k: (y, z + (k if c == 0 else -k), c), shape)
        for k in range(1, deep // 2)
    ]
    here.append(moved(group, lambda y, z, c: (y, z + deep // 2, c), shape))
    return jnp.concatenate(here, axis=0)


def last_swap(both, here, shape):
    other = moved(here, lambda y, z, c: (y, z, c + 1), shape)
    return jnp.concatenate([both, here, other], axis=0)


def ring_shift(values, step, size):
    return lax.ppermute(values, "grid", [(i, (i + step) % size) for i in range(size)])


def unit_rows(values):
    return values * lax.rsqrt(jnp.mean(values * values, axis=-1, keepdims=True) + EPSILON)


def on_device(
    tokens, routes, route_gates, caption_lengths, image_embed, final_gain, up_weight, down_weight
):
    token_count, width = tokens.shape
    experts_all = lax.axis_size("expert")
    grid_all = lax.axis_size("grid")
    slots = 4 * token_count // experts_all
    places_all = experts_all * slots
    scale_root = math.sqrt(width)

    picture_unit = (unit_rows(image_embed.astype(F32)) / scale_root).astype(BF16)
    captions_here = picture_unit.shape[0]
    shape = (grid_all, experts_all // (2 * grid_all), 2)
    row_parts = [picture_unit] + [ring_shift(picture_unit, k, grid_all) for k in range(1, grid_all)]

    stream = tokens.astype(F32)
    normed = layer_norm(stream).astype(BF16)
    first, second = routes[:, 0:1], routes[:, 1:2]
    names = jnp.arange(experts_all, dtype=jnp.int32)[None, :]
    hot_first = first == names
    hot_second = second == names
    both_hot = jnp.concatenate([hot_first, hot_second], axis=1).astype(BF16)
    order = jnp.arange(token_count, dtype=jnp.int32)
    before = (order[None, :] < order[:, None]).astype(BF16)
    ranks = jnp.dot(before, both_hot, preferred_element_type=F32)
    totals = jnp.sum(hot_first.astype(F32), axis=0, keepdims=True)
    rank_first = jnp.sum(jnp.where(hot_first, ranks[:, :experts_all], 0.0), axis=1, keepdims=True)
    rank_second = jnp.sum(
        jnp.where(hot_second, ranks[:, experts_all:] + totals, 0.0), axis=1, keepdims=True
    )
    place_first = first * slots + rank_first.astype(jnp.int32)
    place_second = second * slots + rank_second.astype(jnp.int32)
    spots = jnp.arange(places_all, dtype=jnp.int32)[None, :]
    at_first = spots == place_first
    at_second = spots == place_second
    chosen = (at_first | at_second).astype(BF16)
    send = lax.dot_general(chosen, normed, (((0,), (0,)), ((), ())), preferred_element_type=F32)
    send = send.astype(BF16).reshape(experts_all, slots, width)
    arrived = lax.all_to_all(send, "expert", split_axis=0, concat_axis=0, tiled=True)
    arrived, picture_later, *row_parts = held(arrived, picture_unit, *row_parts)
    pictures_row = jnp.concatenate(row_parts, axis=0)
    rows = arrived.reshape(places_all, width)

    up_local = up_weight[0]
    down_local = down_weight[0]
    from_left = ring_shift(rows, 1, grid_all)
    from_right = ring_shift(rows, -1, grid_all)
    from_far = ring_shift(rows, 2, grid_all)
    own_term = expert_part(rows, up_local, down_local)
    own_term, picture_later = held(own_term, picture_later)
    picture_column = along_expert(picture_later, shape)
    from_left, from_right, own_term = held(from_left, from_right, own_term)
    from_far, picture_column = held(from_far, picture_column)
    back_left = ring_shift(expert_part(from_left, up_local, down_local), -1, grid_all)
    back_right = ring_shift(expert_part(from_right, up_local, down_local), 1, grid_all)
    back_far = ring_shift(expert_part(from_far, up_local, down_local), 2, grid_all)
    total = sum(term.astype(F32) for term in (own_term, back_left, back_right, back_far))
    results = total.astype(BF16).reshape(experts_all, slots, width)
    returned = lax.all_to_all(results, "expert", split_axis=0, concat_axis=0, tiled=True)
    returned = returned.reshape(places_all, width)

    gates = jnp.where(at_first, route_gates[:, 0:1], 0.0) + jnp.where(
        at_second, route_gates[:, 1:2], 0.0
    )
    gate_high, gate_low = split_pair(gates)
    mixed = (
        stream
        + jnp.dot(gate_high, returned, preferred_element_type=F32)
        + jnp.dot(gate_low, returned, preferred_element_type=F32)
    )
    final = layer_norm(mixed) * final_gain
    lengths = caption_lengths[0]
    ends = jnp.cumsum(lengths)
    starts = ends - lengths
    members = ((order[None, :] >= starts[:, None]) & (order[None, :] < ends[:, None])).astype(F32)
    pooled = jnp.dot(members, final, precision=lax.Precision.HIGHEST) / lengths[:, None].astype(F32)
    text_embed = unit_rows(pooled)
    text_unit = (text_embed / scale_root).astype(BF16)

    text_group = along_y(text_unit, shape)
    text_both = on_chip(text_group, shape)
    text_mine, text_both = held(text_unit, text_both)
    text_here = along_z(text_group, text_both, shape)
    text_parts = [text_mine] + [ring_shift(text_mine, k, grid_all) for k in range(1, grid_all)]
    text_column = last_swap(text_both, text_here, shape)
    text_row = jnp.concatenate(text_parts, axis=0)

    def slopes(mine, others, place):
        logits = SIMILARITY_HEAT * lax.dot_general(
            mine, others, (((1,), (1,)), ((), ())), preferred_element_type=F32
        )
        row_ids = lax.broadcasted_iota(jnp.int32, logits.shape, 0)
        column_ids = lax.broadcasted_iota(jnp.int32, logits.shape, 1)
        same = (row_ids < captions_here) & (row_ids + place == column_ids)
        return weighted_sum(pair_slope(logits, same), others)

    chip = lax.axis_index("expert") // shape[2]
    partial = jnp.concatenate(
        [
            slopes(text_row, picture_column, chip * captions_here).reshape(grid_all, captions_here, width),
            slopes(pictures_row, text_column, 0).reshape(grid_all, captions_here, width),
        ],
        axis=1,
    )
    slope = partial[0]
    for k in range(1, grid_all):
        slope = slope + ring_shift(partial[k], -k, grid_all)
    return (text_embed, slope[:captions_here], slope[captions_here:])


def solution(mesh):
    split = P(("expert", "grid"), None)
    weights = P("expert", None, "grid")
    return jax.shard_map(
        on_device,
        mesh=mesh,
        in_specs=(split, split, split, split, split, P(), weights, weights),
        out_specs=(split, split, split),
        check_vma=False,
    )
```

```python
import math

import jax
import jax.numpy as jnp
from jax import lax
from jax.experimental import pallas as pl
from jax.experimental.pallas import tpu as pltpu
from jax.sharding import PartitionSpec as P

EPSILON = 1e-06
SIMILARITY_HEAT = 10.0
BF16 = jnp.bfloat16
F32 = jnp.float32


def layer_norm(values):
    centred = values - jnp.mean(values, axis=-1, keepdims=True)
    return centred * lax.rsqrt(jnp.mean(centred * centred, axis=-1, keepdims=True) + EPSILON)


def expert_kernel(rows_ref, up_ref, down_ref, out_ref, total_ref):
    step = pl.program_id(0)
    hidden = jnp.dot(rows_ref[...], up_ref[...], preferred_element_type=F32)
    hidden = (0.5 * hidden * (1.0 + lax.erf(hidden * math.sqrt(0.5)))).astype(BF16)
    term = lax.dot_general(
        hidden, down_ref[...], (((1,), (1,)), ((), ())), preferred_element_type=F32
    )

    @pl.when(step == 0)
    def _():
        total_ref[...] = term

    @pl.when(step > 0)
    def _():
        total_ref[...] += term

    @pl.when(step == pl.num_programs(0) - 1)
    def _():
        out_ref[...] = total_ref[...].astype(BF16)


def expert_part(rows, up_piece, down_piece):
    count, width = rows.shape
    units = up_piece.shape[1]
    tile = min(256, units)
    return pl.pallas_call(
        expert_kernel,
        grid=(units // tile,),
        in_specs=[
            pl.BlockSpec((count, width), lambda i: (0, 0)),
            pl.BlockSpec((width, tile), lambda i: (0, i)),
            pl.BlockSpec((width, tile), lambda i: (0, i)),
        ],
        out_specs=pl.BlockSpec((count, width), lambda i: (0, 0)),
        out_shape=jax.ShapeDtypeStruct((count, width), BF16),
        scratch_shapes=[pltpu.VMEM((count, width), F32)],
        compiler_params=pltpu.CompilerParams(vmem_limit_bytes=56 * 2**20),
        cost_estimate=pl.CostEstimate(
            flops=16 * count * width * units,
            bytes_accessed=4 * width * units + 4 * count * width,
            transcendentals=count * units,
        ),
    )(rows, up_piece, down_piece)


def split_pair(values):
    high = values.astype(BF16)
    return high, (values - high.astype(F32)).astype(BF16)


def pair_slope(logits, same):
    signs = jnp.where(same, 1.0, -1.0).astype(F32)
    return -signs * jax.nn.sigmoid(-signs * logits)


def weighted_sum(coeff, rows):
    high, low = split_pair(coeff)
    both = jnp.dot(jnp.concatenate([high, low], axis=0), rows, preferred_element_type=F32)
    count = coeff.shape[0]
    return SIMILARITY_HEAT * (both[:count] + both[count:])


def held(*values):
    return lax.optimization_barrier(values)


def moved(values, target, mesh_shape):
    wide, deep, cores = mesh_shape
    pairs = []
    for index in range(wide * deep * cores):
        y, z, core = index // (deep * cores), index // cores % deep, index % cores
        y, z, core = target(y, z, core)
        pairs.append((index, (y % wide * deep + z % deep) * cores + core % cores))
    return lax.ppermute(values, "expert", pairs)


def along_y(mine, shape):
    others = [moved(mine, lambda y, z, c, k=k: (y + k, z, c), shape) for k in range(1, shape[0])]
    return jnp.concatenate([mine] + others, axis=0)


def along_expert(mine, shape):
    wide, deep, cores = shape
    chips = wide * deep
    groups = [[chip * cores + core for chip in range(chips)] for core in range(cores)]
    copies = jnp.broadcast_to(mine[None], (chips,) + mine.shape)
    column = lax.all_to_all(
        copies, "expert", split_axis=0, concat_axis=0, axis_index_groups=groups, tiled=True
    ).reshape(chips * mine.shape[0], mine.shape[1])
    return on_chip(column, shape)


def on_chip(group, shape):
    return jnp.concatenate([group, moved(group, lambda y, z, c: (y, z, c + 1), shape)], axis=0)


def along_z(group, both, shape):
    deep = shape[1]
    here = [
        moved(both, lambda y, z, c, k=k: (y, z + (k if c == 0 else -k), c), shape)
        for k in range(1, deep // 2)
    ]
    here.append(moved(group, lambda y, z, c: (y, z + deep // 2, c), shape))
    return jnp.concatenate(here, axis=0)


def last_swap(both, here, shape):
    other = moved(here, lambda y, z, c: (y, z, c + 1), shape)
    return jnp.concatenate([both, here, other], axis=0)


def ring_shift(values, step, size):
    return lax.ppermute(values, "grid", [(i, (i + step) % size) for i in range(size)])


def unit_rows(values):
    return values * lax.rsqrt(jnp.mean(values * values, axis=-1, keepdims=True) + EPSILON)


def on_device(
    tokens, routes, route_gates, caption_lengths, image_embed, final_gain, up_weight, down_weight
):
    token_count, width = tokens.shape
    experts_all = lax.axis_size("expert")
    grid_all = lax.axis_size("grid")
    slots = 4 * token_count // experts_all
    places_all = experts_all * slots
    scale_root = math.sqrt(width)

    picture_unit = (unit_rows(image_embed.astype(F32)) / scale_root).astype(BF16)
    captions_here = picture_unit.shape[0]
    shape = (grid_all, experts_all // (2 * grid_all), 2)
    chip = lax.axis_index("expert") // shape[2]

    stream = tokens.astype(F32)
    normed = layer_norm(stream).astype(BF16)
    first, second = routes[:, 0:1], routes[:, 1:2]
    names = jnp.arange(experts_all, dtype=jnp.int32)[None, :]
    hot_first = first == names
    hot_second = second == names
    both_hot = jnp.concatenate([hot_first, hot_second], axis=1).astype(BF16)
    order = jnp.arange(token_count, dtype=jnp.int32)
    before = (order[None, :] < order[:, None]).astype(BF16)
    ranks = jnp.dot(before, both_hot, preferred_element_type=F32)
    totals = jnp.sum(hot_first.astype(F32), axis=0, keepdims=True)
    rank_first = jnp.sum(jnp.where(hot_first, ranks[:, :experts_all], 0.0), axis=1, keepdims=True)
    rank_second = jnp.sum(
        jnp.where(hot_second, ranks[:, experts_all:] + totals, 0.0), axis=1, keepdims=True
    )
    place_first = first * slots + rank_first.astype(jnp.int32)
    place_second = second * slots + rank_second.astype(jnp.int32)
    spots = jnp.arange(places_all, dtype=jnp.int32)[None, :]
    at_first = spots == place_first
    at_second = spots == place_second
    chosen = (at_first | at_second).astype(BF16)
    send = lax.dot_general(chosen, normed, (((0,), (0,)), ((), ())), preferred_element_type=F32)
    send = send.astype(BF16).reshape(experts_all, slots, width)
    arrived = lax.all_to_all(send, "expert", split_axis=0, concat_axis=0, tiled=True)
    rows = arrived.reshape(places_all, width)

    up_local = up_weight[0]
    down_local = down_weight[0]
    half = places_all // 2
    top, bottom = rows[:half], rows[half:]
    left_top = ring_shift(top, 1, grid_all)
    right_bottom = ring_shift(bottom, -1, grid_all)
    own_term = expert_part(rows, up_local, down_local)
    own_term, top, bottom = held(own_term, top, bottom)
    left_bottom = ring_shift(bottom, 1, grid_all)
    right_top = ring_shift(top, -1, grid_all)
    far_top = ring_shift(left_top, 1, grid_all)
    far_bottom = ring_shift(right_bottom, -1, grid_all)
    left_top = expert_part(left_top, up_local, down_local)
    right_bottom = expert_part(right_bottom, up_local, down_local)
    far_top = expert_part(far_top, up_local, down_local)
    far_bottom = expert_part(far_bottom, up_local, down_local)
    far_from_left = ring_shift(far_top, 1, grid_all)
    far_from_right = ring_shift(far_bottom, -1, grid_all)
    left_top, right_bottom, far_bottom = held(left_top, right_bottom, far_bottom)
    home_top = ring_shift(left_top, -1, grid_all)
    home_bottom = ring_shift(right_bottom, 1, grid_all)
    right_top = expert_part(right_top, up_local, down_local)
    left_bottom = expert_part(left_bottom, up_local, down_local)
    right_top = (right_top.astype(F32) + far_from_left.astype(F32)).astype(BF16)
    left_bottom = (left_bottom.astype(F32) + far_from_right.astype(F32)).astype(BF16)
    last_top = ring_shift(right_top, 1, grid_all)
    last_bottom = ring_shift(left_bottom, -1, grid_all)
    right_top, left_bottom, picture_later = held(right_top, left_bottom, picture_unit)
    picture_column = along_expert(picture_later, shape)
    total_top = own_term[:half].astype(F32) + home_top.astype(F32) + last_top.astype(F32)
    total_bottom = own_term[half:].astype(F32) + home_bottom.astype(F32) + last_bottom.astype(F32)
    total = jnp.concatenate([total_top, total_bottom], axis=0).astype(BF16)
    total, picture_column = held(total, picture_column)
    results = total.reshape(experts_all, slots, width)
    returned = lax.all_to_all(results, "expert", split_axis=0, concat_axis=0, tiled=True)
    picture_parts = [picture_column] + [
        ring_shift(picture_column, k, grid_all) for k in range(1, grid_all)
    ]
    pictures_all = jnp.concatenate(picture_parts, axis=0)
    pictures_row = lax.dynamic_slice_in_dim(
        jnp.stack(picture_parts), chip * captions_here, captions_here, axis=1
    ).reshape(grid_all * captions_here, width)
    returned, pictures_all, pictures_row = held(returned, pictures_all, pictures_row)
    returned = returned.reshape(places_all, width)

    gates = jnp.where(at_first, route_gates[:, 0:1], 0.0) + jnp.where(
        at_second, route_gates[:, 1:2], 0.0
    )
    gate_high, gate_low = split_pair(gates)
    mixed = (
        stream
        + jnp.dot(gate_high, returned, preferred_element_type=F32)
        + jnp.dot(gate_low, returned, preferred_element_type=F32)
    )
    final = layer_norm(mixed) * final_gain
    lengths = caption_lengths[0]
    ends = jnp.cumsum(lengths)
    starts = ends - lengths
    members = ((order[None, :] >= starts[:, None]) & (order[None, :] < ends[:, None])).astype(F32)
    pooled = jnp.dot(members, final, precision=lax.Precision.HIGHEST) / lengths[:, None].astype(F32)
    text_embed = unit_rows(pooled)
    text_unit = (text_embed / scale_root).astype(BF16)

    text_group = along_y(text_unit, shape)
    text_both = on_chip(text_group, shape)
    text_here = along_z(text_group, text_both, shape)
    text_column = last_swap(text_both, text_here, shape)

    def slopes(mine, others, place):
        logits = SIMILARITY_HEAT * lax.dot_general(
            mine, others, (((1,), (1,)), ((), ())), preferred_element_type=F32
        )
        row_ids = lax.broadcasted_iota(jnp.int32, logits.shape, 0)
        column_ids = lax.broadcasted_iota(jnp.int32, logits.shape, 1)
        same = (row_ids < captions_here) & (row_ids + place == column_ids)
        return weighted_sum(pair_slope(logits, same), others)

    sentence_slope = slopes(text_unit, pictures_all, chip * captions_here)
    partial = slopes(pictures_row, text_column, 0).reshape(grid_all, captions_here, width)
    picture_slope = partial[0]
    for k in range(1, grid_all):
        picture_slope = picture_slope + ring_shift(partial[k], -k, grid_all)
    return (text_embed, sentence_slope, picture_slope)


def solution(mesh):
    split = P(("expert", "grid"), None)
    weights = P("expert", None, "grid")
    return jax.shard_map(
        on_device,
        mesh=mesh,
        in_specs=(split, split, split, split, split, P(), weights, weights),
        out_specs=(split, split, split),
        check_vma=False,
    )
```

```python
import functools
import math

import jax
import jax.numpy as jnp
from jax import lax
from jax.experimental import pallas as pl
from jax.experimental.pallas import tpu as pltpu
from jax.sharding import PartitionSpec as P

EPSILON = 1e-06
SIMILARITY_HEAT = 10.0
BF16 = jnp.bfloat16
F32 = jnp.float32


def layer_norm(values):
    centred = values - jnp.mean(values, axis=-1, keepdims=True)
    return centred * lax.rsqrt(jnp.mean(centred * centred, axis=-1, keepdims=True) + EPSILON)


def expert_kernel(*refs):
    blocks = (len(refs) - 3) // 2
    rows_refs, (up_ref, down_ref) = refs[:blocks], refs[blocks : blocks + 2]
    out_refs, total_ref = refs[blocks + 2 : -1], refs[-1]
    step = pl.program_id(0)
    rows = jnp.concatenate([ref[...] for ref in rows_refs], axis=0)
    hidden = jnp.dot(rows, up_ref[...], preferred_element_type=F32)
    hidden = (0.5 * hidden * (1.0 + lax.erf(hidden * math.sqrt(0.5)))).astype(BF16)
    term = lax.dot_general(
        hidden, down_ref[...], (((1,), (1,)), ((), ())), preferred_element_type=F32
    )

    @pl.when(step == 0)
    def _():
        total_ref[...] = term

    @pl.when(step > 0)
    def _():
        total_ref[...] += term

    @pl.when(step == pl.num_programs(0) - 1)
    def _():
        start = 0
        for ref in out_refs:
            ref[...] = total_ref[start : start + ref.shape[0], :].astype(BF16)
            start += ref.shape[0]


def expert_part(blocks, up_piece, down_piece):
    width, units = up_piece.shape
    count = sum(block.shape[0] for block in blocks)
    tile = min(256, units)
    whole = [pl.BlockSpec(block.shape, lambda i: (0, 0)) for block in blocks]
    return pl.pallas_call(
        expert_kernel,
        grid=(units // tile,),
        in_specs=whole
        + [
            pl.BlockSpec((width, tile), lambda i: (0, i)),
            pl.BlockSpec((width, tile), lambda i: (0, i)),
        ],
        out_specs=whole,
        out_shape=[jax.ShapeDtypeStruct(block.shape, BF16) for block in blocks],
        scratch_shapes=[pltpu.VMEM((count, width), F32)],
        compiler_params=pltpu.CompilerParams(vmem_limit_bytes=56 * 2**20),
        cost_estimate=pl.CostEstimate(
            flops=16 * count * width * units,
            bytes_accessed=4 * width * units + 4 * count * width,
            transcendentals=count * units,
        ),
    )(*blocks, up_piece, down_piece)


def sum_kernel(own_ref, home_top, last_top, home_bottom, last_bottom, out_ref):
    own = own_ref[...].astype(F32)
    early = pl.program_id(0) < pl.num_programs(0) // 2

    @pl.when(early)
    def _():
        out_ref[...] = (own + home_top[...].astype(F32) + last_top[...].astype(F32)).astype(BF16)

    @pl.when(jnp.logical_not(early))
    def _():
        out_ref[...] = (
            own + home_bottom[...].astype(F32) + last_bottom[...].astype(F32)
        ).astype(BF16)


def sum_terms(own, home_top, last_top, home_bottom, last_bottom):
    count, width = own.shape
    steps = 4
    block = (count // steps, width)
    top = pl.BlockSpec(block, lambda i: (jnp.minimum(i, steps // 2 - 1), 0))
    bottom = pl.BlockSpec(block, lambda i: (jnp.maximum(i - steps // 2, 0), 0))
    return pl.pallas_call(
        sum_kernel,
        grid=(steps,),
        in_specs=[pl.BlockSpec(block, lambda i: (i, 0)), top, top, bottom, bottom],
        out_specs=pl.BlockSpec(block, lambda i: (i, 0)),
        out_shape=jax.ShapeDtypeStruct(own.shape, BF16),
        compiler_params=pltpu.CompilerParams(vmem_limit_bytes=16 * 2**20),
    )(own, home_top, last_top, home_bottom, last_bottom)


def dispatch_kernel(slots, tokens_ref, routes_ref, send_ref, place_ref):
    count = tokens_ref.shape[0]
    places = send_ref.shape[0]
    normed = layer_norm(tokens_ref[...].astype(F32)).astype(BF16)
    first, second = routes_ref[:, 0:1], routes_ref[:, 1:2]
    names = lax.broadcasted_iota(jnp.int32, (count, places // slots), 1)
    hot_first = (first == names).astype(F32)
    hot_second = (second == names).astype(F32)
    row_ids = lax.broadcasted_iota(jnp.int32, (count, count), 0)
    before = (lax.broadcasted_iota(jnp.int32, (count, count), 1) < row_ids).astype(F32).astype(BF16)
    rank_first = jnp.dot(before, hot_first.astype(BF16), preferred_element_type=F32)
    rank_second = jnp.dot(before, hot_second.astype(BF16), preferred_element_type=F32)
    rank_second = rank_second + jnp.sum(hot_first, axis=0, keepdims=True)
    rank_first = jnp.sum(rank_first * hot_first, axis=1, keepdims=True)
    rank_second = jnp.sum(rank_second * hot_second, axis=1, keepdims=True)
    place_first = first * slots + rank_first.astype(jnp.int32)
    place_second = second * slots + rank_second.astype(jnp.int32)
    place_ref[:, 0:1] = place_first
    place_ref[:, 1:2] = place_second
    spots = lax.broadcasted_iota(jnp.int32, (count, places), 1)
    chosen = ((spots == place_first) | (spots == place_second)).astype(F32)
    send = jnp.dot(chosen.T.astype(BF16), normed, preferred_element_type=F32)
    send_ref[...] = send.astype(BF16)


def dispatch(tokens, routes, places, slots):
    return pl.pallas_call(
        functools.partial(dispatch_kernel, slots),
        out_shape=[
            jax.ShapeDtypeStruct((places, tokens.shape[1]), BF16),
            jax.ShapeDtypeStruct(routes.shape, jnp.int32),
        ],
        compiler_params=pltpu.CompilerParams(vmem_limit_bytes=16 * 2**20),
    )(tokens, routes)


def split_pair(values):
    high = values.astype(BF16)
    return high, (values - high.astype(F32)).astype(BF16)


def pair_slope(logits, same):
    signs = jnp.where(same, 1.0, -1.0).astype(F32)
    return -signs * jax.nn.sigmoid(-signs * logits)


def weighted_sum(coeff, rows):
    high, low = split_pair(coeff)
    both = jnp.dot(jnp.concatenate([high, low], axis=0), rows, preferred_element_type=F32)
    count = coeff.shape[0]
    return SIMILARITY_HEAT * (both[:count] + both[count:])


def held(*values):
    return lax.optimization_barrier(values)


def moved(values, target, mesh_shape):
    wide, deep, cores = mesh_shape
    pairs = []
    for index in range(wide * deep * cores):
        y, z, core = index // (deep * cores), index // cores % deep, index % cores
        y, z, core = target(y, z, core)
        pairs.append((index, (y % wide * deep + z % deep) * cores + core % cores))
    return lax.ppermute(values, "expert", pairs)


def along_expert(mine, shape):
    wide, deep, cores = shape
    chips = wide * deep
    groups = [[chip * cores + core for chip in range(chips)] for core in range(cores)]
    copies = jnp.broadcast_to(mine[None], (chips,) + mine.shape)
    column = lax.all_to_all(
        copies, "expert", split_axis=0, concat_axis=0, axis_index_groups=groups, tiled=True
    ).reshape(chips * mine.shape[0], mine.shape[1])
    return on_chip(column, shape)


def on_chip(group, shape):
    return jnp.concatenate([group, moved(group, lambda y, z, c: (y, z, c + 1), shape)], axis=0)


def ring_shift(values, step, size):
    return lax.ppermute(values, "grid", [(i, (i + step) % size) for i in range(size)])


def unit_rows(values):
    return values * lax.rsqrt(jnp.mean(values * values, axis=-1, keepdims=True) + EPSILON)


def on_device(
    tokens, routes, route_gates, caption_lengths, image_embed, final_gain, up_weight, down_weight
):
    token_count, width = tokens.shape
    experts_all = lax.axis_size("expert")
    grid_all = lax.axis_size("grid")
    slots = 4 * token_count // experts_all
    places_all = experts_all * slots
    scale_root = math.sqrt(width)

    picture_unit = (unit_rows(image_embed.astype(F32)) / scale_root).astype(BF16)
    captions_here = picture_unit.shape[0]
    shape = (grid_all, experts_all // (2 * grid_all), 2)
    chip = lax.axis_index("expert") // shape[2]

    stream = tokens.astype(F32)
    send, place = dispatch(tokens, routes, places_all, slots)
    spots = jnp.arange(places_all, dtype=jnp.int32)[None, :]
    at_first = spots == place[:, 0:1]
    at_second = spots == place[:, 1:2]
    order = jnp.arange(token_count, dtype=jnp.int32)
    send = send.reshape(experts_all, slots, width)
    arrived = lax.all_to_all(send, "expert", split_axis=0, concat_axis=0, tiled=True)
    rows = arrived.reshape(places_all, width)

    up_local = up_weight[0]
    down_local = down_weight[0]
    half = places_all // 2
    top, bottom = rows[:half], rows[half:]
    left_top = ring_shift(top, 1, grid_all)
    right_bottom = ring_shift(bottom, -1, grid_all)
    own_term = expert_part([rows], up_local, down_local)[0]
    own_term, top, bottom, left_top, right_bottom = held(
        own_term, top, bottom, left_top, right_bottom
    )
    left_bottom = ring_shift(bottom, 1, grid_all)
    right_top = ring_shift(top, -1, grid_all)
    far_top = ring_shift(left_top, 1, grid_all)
    far_bottom = ring_shift(right_bottom, -1, grid_all)
    left_top, right_bottom = expert_part([left_top, right_bottom], up_local, down_local)
    home_top = ring_shift(left_top, -1, grid_all)
    home_bottom = ring_shift(right_bottom, 1, grid_all)
    right_top, left_bottom, left_top, right_bottom = held(
        right_top, left_bottom, left_top, right_bottom
    )
    right_top, left_bottom = expert_part([right_top, left_bottom], up_local, down_local)
    far_top, far_bottom, left_top, right_bottom, right_top, left_bottom = held(
        far_top, far_bottom, left_top, right_bottom, right_top, left_bottom
    )
    far_top, far_bottom = expert_part([far_top, far_bottom], up_local, down_local)
    far_from_left = ring_shift(far_top, 1, grid_all)
    far_from_right = ring_shift(far_bottom, -1, grid_all)
    far_from_left, far_from_right, home_top, home_bottom = held(
        far_from_left, far_from_right, home_top, home_bottom
    )
    right_top = (right_top.astype(F32) + far_from_left.astype(F32)).astype(BF16)
    left_bottom = (left_bottom.astype(F32) + far_from_right.astype(F32)).astype(BF16)
    last_top = ring_shift(right_top, 1, grid_all)
    last_bottom = ring_shift(left_bottom, -1, grid_all)
    right_top, left_bottom, picture_later = held(right_top, left_bottom, picture_unit)
    picture_column = along_expert(picture_later, shape)
    total = sum_terms(own_term, home_top, last_top, home_bottom, last_bottom)
    total, picture_column = held(total, picture_column)
    results = total.reshape(experts_all, slots, width)
    returned = lax.all_to_all(results, "expert", split_axis=0, concat_axis=0, tiled=True)
    picture_parts = [picture_column] + [
        ring_shift(picture_column, k, grid_all) for k in range(1, grid_all)
    ]
    pictures_all = jnp.concatenate(picture_parts, axis=0)
    pictures_row = lax.dynamic_slice_in_dim(
        jnp.stack(picture_parts), chip * captions_here, captions_here, axis=1
    ).reshape(grid_all * captions_here, width)
    returned, pictures_all, pictures_row = held(returned, pictures_all, pictures_row)
    returned = returned.reshape(places_all, width)

    gates = jnp.where(at_first, route_gates[:, 0:1], 0.0) + jnp.where(
        at_second, route_gates[:, 1:2], 0.0
    )
    gate_high, gate_low = split_pair(gates)
    mixed = (
        stream
        + jnp.dot(gate_high, returned, preferred_element_type=F32)
        + jnp.dot(gate_low, returned, preferred_element_type=F32)
    )
    final = layer_norm(mixed) * final_gain
    lengths = caption_lengths[0]
    ends = jnp.cumsum(lengths)
    starts = ends - lengths
    members = ((order[None, :] >= starts[:, None]) & (order[None, :] < ends[:, None])).astype(F32)
    pooled = jnp.dot(members, final, precision=lax.Precision.HIGHEST) / lengths[:, None].astype(F32)
    text_embed = unit_rows(pooled)
    text_unit = (text_embed / scale_root).astype(BF16)

    text_column = along_expert(text_unit, shape)

    def slopes(mine, others, place):
        logits = SIMILARITY_HEAT * lax.dot_general(
            mine, others, (((1,), (1,)), ((), ())), preferred_element_type=F32
        )
        row_ids = lax.broadcasted_iota(jnp.int32, logits.shape, 0)
        column_ids = lax.broadcasted_iota(jnp.int32, logits.shape, 1)
        same = (row_ids < captions_here) & (row_ids + place == column_ids)
        return weighted_sum(pair_slope(logits, same), others)

    sentence_slope = slopes(text_unit, pictures_all, chip * captions_here)
    partial = slopes(pictures_row, text_column, chip * captions_here).reshape(grid_all, captions_here, width)
    picture_slope = partial[0]
    for k in range(1, grid_all):
        picture_slope = picture_slope + ring_shift(partial[k], -k, grid_all)
    return (text_embed, sentence_slope, picture_slope)


def solution(mesh):
    split = P(("expert", "grid"), None)
    weights = P("expert", None, "grid")
    return jax.shard_map(
        on_device,
        mesh=mesh,
        in_specs=(split, split, split, split, split, P(), weights, weights),
        out_specs=(split, split, split),
        check_vma=False,
    )
```

```python
import functools
import math

import jax
import jax.numpy as jnp
from jax import lax
from jax.experimental import pallas as pl
from jax.experimental.pallas import tpu as pltpu
from jax.sharding import PartitionSpec as P

EPSILON = 1e-06
SIMILARITY_HEAT = 10.0
BF16 = jnp.bfloat16
F32 = jnp.float32


def layer_norm(values):
    centred = values - jnp.mean(values, axis=-1, keepdims=True)
    return centred * lax.rsqrt(jnp.mean(centred * centred, axis=-1, keepdims=True) + EPSILON)


def expert_kernel(*refs):
    blocks = (len(refs) - 3) // 2
    rows_refs, (up_ref, down_ref) = refs[:blocks], refs[blocks : blocks + 2]
    out_refs, total_ref = refs[blocks + 2 : -1], refs[-1]
    step = pl.program_id(0)
    rows = jnp.concatenate([ref[...] for ref in rows_refs], axis=0)
    hidden = jnp.dot(rows, up_ref[...], preferred_element_type=F32)
    hidden = (0.5 * hidden * (1.0 + lax.erf(hidden * math.sqrt(0.5)))).astype(BF16)
    term = lax.dot_general(
        hidden, down_ref[...], (((1,), (1,)), ((), ())), preferred_element_type=F32
    )

    @pl.when(step == 0)
    def _():
        total_ref[...] = term

    @pl.when(step > 0)
    def _():
        total_ref[...] += term

    @pl.when(step == pl.num_programs(0) - 1)
    def _():
        start = 0
        for ref in out_refs:
            ref[...] = total_ref[start : start + ref.shape[0], :].astype(BF16)
            start += ref.shape[0]


def expert_part(blocks, up_piece, down_piece):
    width, units = up_piece.shape
    count = sum(block.shape[0] for block in blocks)
    tile = min(256, units)
    whole = [pl.BlockSpec(block.shape, lambda i: (0, 0)) for block in blocks]
    return pl.pallas_call(
        expert_kernel,
        grid=(units // tile,),
        in_specs=whole
        + [
            pl.BlockSpec((width, tile), lambda i: (0, i)),
            pl.BlockSpec((width, tile), lambda i: (0, i)),
        ],
        out_specs=whole,
        out_shape=[jax.ShapeDtypeStruct(block.shape, BF16) for block in blocks],
        scratch_shapes=[pltpu.VMEM((count, width), F32)],
        compiler_params=pltpu.CompilerParams(vmem_limit_bytes=56 * 2**20),
        cost_estimate=pl.CostEstimate(
            flops=16 * count * width * units,
            bytes_accessed=4 * width * units + 4 * count * width,
            transcendentals=count * units,
        ),
    )(*blocks, up_piece, down_piece)


def sum_kernel(own_ref, home_top, last_top, home_bottom, last_bottom, out_ref):
    own = own_ref[...].astype(F32)
    early = pl.program_id(0) < pl.num_programs(0) // 2

    @pl.when(early)
    def _():
        out_ref[...] = (own + home_top[...].astype(F32) + last_top[...].astype(F32)).astype(BF16)

    @pl.when(jnp.logical_not(early))
    def _():
        out_ref[...] = (
            own + home_bottom[...].astype(F32) + last_bottom[...].astype(F32)
        ).astype(BF16)


def sum_terms(own, home_top, last_top, home_bottom, last_bottom):
    count, width = own.shape
    steps = 4
    block = (count // steps, width)
    top = pl.BlockSpec(block, lambda i: (jnp.minimum(i, steps // 2 - 1), 0))
    bottom = pl.BlockSpec(block, lambda i: (jnp.maximum(i - steps // 2, 0), 0))
    return pl.pallas_call(
        sum_kernel,
        grid=(steps,),
        in_specs=[pl.BlockSpec(block, lambda i: (i, 0)), top, top, bottom, bottom],
        out_specs=pl.BlockSpec(block, lambda i: (i, 0)),
        out_shape=jax.ShapeDtypeStruct(own.shape, BF16),
        compiler_params=pltpu.CompilerParams(vmem_limit_bytes=16 * 2**20),
    )(own, home_top, last_top, home_bottom, last_bottom)


def dispatch_kernel(slots, tokens_ref, routes_ref, send_ref, place_ref):
    count = tokens_ref.shape[0]
    places = send_ref.shape[0]
    normed = layer_norm(tokens_ref[...].astype(F32)).astype(BF16)
    first, second = routes_ref[:, 0:1], routes_ref[:, 1:2]
    names = lax.broadcasted_iota(jnp.int32, (count, places // slots), 1)
    hot_first = (first == names).astype(F32)
    hot_second = (second == names).astype(F32)
    row_ids = lax.broadcasted_iota(jnp.int32, (count, count), 0)
    before = (lax.broadcasted_iota(jnp.int32, (count, count), 1) < row_ids).astype(F32).astype(BF16)
    rank_first = jnp.dot(before, hot_first.astype(BF16), preferred_element_type=F32)
    rank_second = jnp.dot(before, hot_second.astype(BF16), preferred_element_type=F32)
    rank_second = rank_second + jnp.sum(hot_first, axis=0, keepdims=True)
    rank_first = jnp.sum(rank_first * hot_first, axis=1, keepdims=True)
    rank_second = jnp.sum(rank_second * hot_second, axis=1, keepdims=True)
    place_first = first * slots + rank_first.astype(jnp.int32)
    place_second = second * slots + rank_second.astype(jnp.int32)
    place_ref[:, 0:1] = place_first
    place_ref[:, 1:2] = place_second
    spots = lax.broadcasted_iota(jnp.int32, (count, places), 1)
    chosen = ((spots == place_first) | (spots == place_second)).astype(F32)
    send = jnp.dot(chosen.T.astype(BF16), normed, preferred_element_type=F32)
    send_ref[...] = send.astype(BF16)


def dispatch(tokens, routes, places, slots):
    return pl.pallas_call(
        functools.partial(dispatch_kernel, slots),
        out_shape=[
            jax.ShapeDtypeStruct((places, tokens.shape[1]), BF16),
            jax.ShapeDtypeStruct(routes.shape, jnp.int32),
        ],
        compiler_params=pltpu.CompilerParams(vmem_limit_bytes=16 * 2**20),
    )(tokens, routes)


def combine_kernel(
    lengths_ref, returned_ref, tokens_ref, place_ref, gates_ref, gain_ref, embed_ref, copies_ref
):
    count = tokens_ref.shape[0]
    captions = embed_ref.shape[0]
    returned = returned_ref[...]
    spots = lax.broadcasted_iota(jnp.int32, (count, returned.shape[0]), 1)
    gates = jnp.where(spots == place_ref[:, 0:1], gates_ref[:, 0:1], 0.0) + jnp.where(
        spots == place_ref[:, 1:2], gates_ref[:, 1:2], 0.0
    )
    high, low = split_pair(gates)
    mixed = tokens_ref[...].astype(F32)
    mixed += jnp.dot(high, returned, preferred_element_type=F32)
    mixed += jnp.dot(low, returned, preferred_element_type=F32)
    final = layer_norm(mixed) * gain_ref[...]
    padded = 8
    caption = lax.broadcasted_iota(jnp.int32, (padded, count), 0)
    token = lax.broadcasted_iota(jnp.int32, (padded, count), 1)
    row = lax.broadcasted_iota(jnp.int32, (padded, 1), 0)
    inside = jnp.zeros((padded, count), F32)
    sizes = jnp.ones((padded, 1), F32)
    start = jnp.int32(0)
    for index in range(captions):
        size = lengths_ref[0, index]
        here = (caption == index) & (token >= start) & (token < start + size)
        inside = jnp.where(here, 1.0, inside)
        sizes = jnp.where(row == index, size.astype(F32), sizes)
        start = start + size
    inside = inside.astype(BF16)
    first, rest = final.astype(BF16), final
    pooled = jnp.dot(inside, first, preferred_element_type=F32)
    for _ in range(2):
        rest = rest - first.astype(F32)
        first = rest.astype(BF16)
        pooled += jnp.dot(inside, first, preferred_element_type=F32)
    embed = unit_rows(pooled / sizes)[:captions]
    embed_ref[...] = embed
    unit = (embed * (1.0 / math.sqrt(embed.shape[1]))).astype(BF16)
    copies_ref[...] = jnp.broadcast_to(unit[None], copies_ref.shape)


def combine(lengths, returned, tokens, place, gates, gain, copies):
    captions = lengths.shape[1]
    width = tokens.shape[1]
    vmem = pl.BlockSpec(memory_space=pltpu.VMEM)
    return pl.pallas_call(
        combine_kernel,
        in_specs=[pl.BlockSpec(memory_space=pltpu.SMEM)] + [vmem] * 5,
        out_specs=[vmem, vmem],
        out_shape=[
            jax.ShapeDtypeStruct((captions, width), F32),
            jax.ShapeDtypeStruct((copies, captions, width), BF16),
        ],
        compiler_params=pltpu.CompilerParams(vmem_limit_bytes=24 * 2**20),
    )(lengths, returned, tokens, place, gates, gain.reshape(1, width))


def split_pair(values):
    high = values.astype(BF16)
    return high, (values - high.astype(F32)).astype(BF16)


def pair_slope(logits, same):
    signs = jnp.where(same, 1.0, -1.0).astype(F32)
    return -signs * jax.nn.sigmoid(-signs * logits)


def weighted_sum(coeff, rows):
    high, low = split_pair(coeff)
    both = jnp.dot(jnp.concatenate([high, low], axis=0), rows, preferred_element_type=F32)
    count = coeff.shape[0]
    return SIMILARITY_HEAT * (both[:count] + both[count:])


def held(*values):
    return lax.optimization_barrier(values)


def moved(values, target, mesh_shape):
    wide, deep, cores = mesh_shape
    pairs = []
    for index in range(wide * deep * cores):
        y, z, core = index // (deep * cores), index // cores % deep, index % cores
        y, z, core = target(y, z, core)
        pairs.append((index, (y % wide * deep + z % deep) * cores + core % cores))
    return lax.ppermute(values, "expert", pairs)


def along_expert(copies, shape):
    wide, deep, cores = shape
    chips = wide * deep
    groups = [[chip * cores + core for chip in range(chips)] for core in range(cores)]
    column = lax.all_to_all(
        copies, "expert", split_axis=0, concat_axis=0, axis_index_groups=groups, tiled=True
    ).reshape(chips * copies.shape[1], copies.shape[2])
    return on_chip(column, shape)


def on_chip(group, shape):
    return jnp.concatenate([group, moved(group, lambda y, z, c: (y, z, c + 1), shape)], axis=0)


def ring_shift(values, step, size):
    return lax.ppermute(values, "grid", [(i, (i + step) % size) for i in range(size)])


def unit_rows(values):
    return values * lax.rsqrt(jnp.mean(values * values, axis=-1, keepdims=True) + EPSILON)


def on_device(
    tokens, routes, route_gates, caption_lengths, image_embed, final_gain, up_weight, down_weight
):
    token_count, width = tokens.shape
    experts_all = lax.axis_size("expert")
    grid_all = lax.axis_size("grid")
    slots = 4 * token_count // experts_all
    places_all = experts_all * slots
    scale_root = math.sqrt(width)

    picture_unit = (unit_rows(image_embed.astype(F32)) / scale_root).astype(BF16)
    captions_here = picture_unit.shape[0]
    shape = (grid_all, experts_all // (2 * grid_all), 2)
    chip = lax.axis_index("expert") // shape[2]

    row_parts = [picture_unit] + [ring_shift(picture_unit, k, grid_all) for k in range(1, grid_all)]
    send, place = dispatch(tokens, routes, places_all, slots)
    send = send.reshape(experts_all, slots, width)
    arrived = lax.all_to_all(send, "expert", split_axis=0, concat_axis=0, tiled=True)
    pictures_row = jnp.concatenate(row_parts, axis=0)
    chips = shape[0] * shape[1]
    picture_copies = jnp.broadcast_to(pictures_row[None], (chips,) + pictures_row.shape)
    arrived, picture_copies, pictures_row = held(arrived, picture_copies, pictures_row)
    rows = arrived.reshape(places_all, width)

    up_local = up_weight[0]
    down_local = down_weight[0]
    half = places_all // 2
    top, bottom = rows[:half], rows[half:]
    left_top = ring_shift(top, 1, grid_all)
    right_bottom = ring_shift(bottom, -1, grid_all)
    pictures_all = along_expert(picture_copies, shape)
    left_bottom = ring_shift(bottom, 1, grid_all)
    right_top = ring_shift(top, -1, grid_all)
    own_term = expert_part([rows], up_local, down_local)[0]
    own_term, left_top, right_bottom = held(own_term, left_top, right_bottom)
    far_top = ring_shift(left_top, 1, grid_all)
    far_bottom = ring_shift(right_bottom, -1, grid_all)
    left_top, right_bottom = expert_part([left_top, right_bottom], up_local, down_local)
    home_top = ring_shift(left_top, -1, grid_all)
    home_bottom = ring_shift(right_bottom, 1, grid_all)
    right_top, left_bottom, left_top, right_bottom = held(
        right_top, left_bottom, left_top, right_bottom
    )
    right_top, left_bottom = expert_part([right_top, left_bottom], up_local, down_local)
    far_top, far_bottom, left_top, right_bottom, right_top, left_bottom = held(
        far_top, far_bottom, left_top, right_bottom, right_top, left_bottom
    )
    far_top, far_bottom = expert_part([far_top, far_bottom], up_local, down_local)
    far_from_left = ring_shift(far_top, 1, grid_all)
    far_from_right = ring_shift(far_bottom, -1, grid_all)
    far_from_left, far_from_right, home_top, home_bottom, pictures_all = held(
        far_from_left, far_from_right, home_top, home_bottom, pictures_all
    )
    right_top = (right_top.astype(F32) + far_from_left.astype(F32)).astype(BF16)
    left_bottom = (left_bottom.astype(F32) + far_from_right.astype(F32)).astype(BF16)
    last_top = ring_shift(right_top, 1, grid_all)
    last_bottom = ring_shift(left_bottom, -1, grid_all)
    total = sum_terms(own_term, home_top, last_top, home_bottom, last_bottom)
    results = total.reshape(experts_all, slots, width)
    returned = lax.all_to_all(results, "expert", split_axis=0, concat_axis=0, tiled=True)
    returned = returned.reshape(places_all, width)

    text_embed, text_copies = combine(
        caption_lengths, returned, tokens, place, route_gates, final_gain, chips
    )
    text_unit = text_copies[0]
    text_column = along_expert(text_copies, shape)

    def slopes(mine, others, place):
        logits = SIMILARITY_HEAT * lax.dot_general(
            mine, others, (((1,), (1,)), ((), ())), preferred_element_type=F32
        )
        row_ids = lax.broadcasted_iota(jnp.int32, logits.shape, 0)
        column_ids = lax.broadcasted_iota(jnp.int32, logits.shape, 1)
        same = (row_ids < captions_here) & (row_ids + place == column_ids)
        return weighted_sum(pair_slope(logits, same), others)

    sentence_slope = slopes(text_unit, pictures_all, chip * pictures_row.shape[0])
    partial = slopes(pictures_row, text_column, chip * captions_here).reshape(grid_all, captions_here, width)
    picture_slope = partial[0]
    for k in range(1, grid_all):
        picture_slope = picture_slope + ring_shift(partial[k], -k, grid_all)
    return (text_embed, sentence_slope, picture_slope)


def solution(mesh):
    split = P(("expert", "grid"), None)
    weights = P("expert", None, "grid")

    return jax.shard_map(
        on_device,
        mesh=mesh,
        in_specs=(split, split, split, split, split, P(), weights, weights),
        out_specs=(split, split, split),
        check_vma=False,
    )
```

```python
import functools
import math

import jax
import jax.numpy as jnp
from jax import lax
from jax.experimental import pallas as pl
from jax.experimental.pallas import tpu as pltpu
from jax.sharding import PartitionSpec as P

EPSILON = 1e-06
SIMILARITY_HEAT = 10.0
BF16 = jnp.bfloat16
F32 = jnp.float32


def layer_norm(values):
    centred = values - jnp.mean(values, axis=-1, keepdims=True)
    return centred * lax.rsqrt(jnp.mean(centred * centred, axis=-1, keepdims=True) + EPSILON)


def expert_kernel(*refs):
    blocks = (len(refs) - 3) // 2
    rows_refs, (up_ref, down_ref) = refs[:blocks], refs[blocks : blocks + 2]
    out_refs, hidden_ref = refs[blocks + 2 : -1], refs[-1]
    step = pl.program_id(0)
    half = pl.num_programs(0) // 2
    tile = up_ref.shape[1]

    @pl.when(step < half)
    def _():
        rows = jnp.concatenate([ref[...] for ref in rows_refs], axis=0)
        hidden = jnp.dot(rows, up_ref[...], preferred_element_type=F32)
        hidden = (0.5 * hidden * (1.0 + lax.erf(hidden * math.sqrt(0.5)))).astype(BF16)
        hidden_ref[:, pl.ds(pl.multiple_of(step * tile, tile), tile)] = hidden

    @pl.when(step >= half)
    def _():
        term = lax.dot_general(
            hidden_ref[...], down_ref[...], (((1,), (1,)), ((), ())), preferred_element_type=F32
        ).astype(BF16)
        start = 0
        for ref in out_refs:
            ref[...] = term[start : start + ref.shape[0]]
            start += ref.shape[0]


def expert_part(blocks, up_piece, down_piece):
    width, units = up_piece.shape
    count = sum(block.shape[0] for block in blocks)
    tile = min(512, units)
    half = units // tile
    return pl.pallas_call(
        expert_kernel,
        grid=(2 * half,),
        in_specs=[pl.BlockSpec(block.shape, lambda i: (0, 0)) for block in blocks]
        + [
            pl.BlockSpec((width, tile), lambda i: (0, jnp.minimum(i, half - 1))),
            pl.BlockSpec((width // half, units), lambda i: (jnp.maximum(i - half, 0), 0)),
        ],
        out_specs=[
            pl.BlockSpec((block.shape[0], width // half), lambda i: (0, jnp.maximum(i - half, 0)))
            for block in blocks
        ],
        out_shape=[jax.ShapeDtypeStruct(block.shape, BF16) for block in blocks],
        scratch_shapes=[pltpu.VMEM((count, units), BF16)],
        compiler_params=pltpu.CompilerParams(vmem_limit_bytes=56 * 2**20),
        cost_estimate=pl.CostEstimate(
            flops=12 * count * width * units,
            bytes_accessed=4 * width * units + 4 * count * width,
            transcendentals=count * units,
        ),
    )(*blocks, up_piece, down_piece)


def sum_kernel(own_ref, home_top, last_top, home_bottom, last_bottom, out_ref):
    own = own_ref[...].astype(F32)
    early = pl.program_id(0) < pl.num_programs(0) // 2

    @pl.when(early)
    def _():
        out_ref[...] = (own + home_top[...].astype(F32) + last_top[...].astype(F32)).astype(BF16)

    @pl.when(jnp.logical_not(early))
    def _():
        out_ref[...] = (
            own + home_bottom[...].astype(F32) + last_bottom[...].astype(F32)
        ).astype(BF16)


def sum_terms(own, home_top, last_top, home_bottom, last_bottom):
    count, width = own.shape
    steps = 4
    block = (count // steps, width)
    top = pl.BlockSpec(block, lambda i: (jnp.minimum(i, steps // 2 - 1), 0))
    bottom = pl.BlockSpec(block, lambda i: (jnp.maximum(i - steps // 2, 0), 0))
    return pl.pallas_call(
        sum_kernel,
        grid=(steps,),
        in_specs=[pl.BlockSpec(block, lambda i: (i, 0)), top, top, bottom, bottom],
        out_specs=pl.BlockSpec(block, lambda i: (i, 0)),
        out_shape=jax.ShapeDtypeStruct(own.shape, BF16),
        compiler_params=pltpu.CompilerParams(vmem_limit_bytes=16 * 2**20),
    )(own, home_top, last_top, home_bottom, last_bottom)


def dispatch_kernel(slots, tokens_ref, routes_ref, send_ref, place_ref):
    count = tokens_ref.shape[0]
    places = send_ref.shape[0]
    normed = layer_norm(tokens_ref[...].astype(F32)).astype(BF16)
    first, second = routes_ref[:, 0:1], routes_ref[:, 1:2]
    names = lax.broadcasted_iota(jnp.int32, (count, places // slots), 1)
    hot_first = (first == names).astype(F32)
    hot_second = (second == names).astype(F32)
    row_ids = lax.broadcasted_iota(jnp.int32, (count, count), 0)
    before = (lax.broadcasted_iota(jnp.int32, (count, count), 1) < row_ids).astype(F32).astype(BF16)
    rank_first = jnp.dot(before, hot_first.astype(BF16), preferred_element_type=F32)
    rank_second = jnp.dot(before, hot_second.astype(BF16), preferred_element_type=F32)
    rank_second = rank_second + jnp.sum(hot_first, axis=0, keepdims=True)
    rank_first = jnp.sum(rank_first * hot_first, axis=1, keepdims=True)
    rank_second = jnp.sum(rank_second * hot_second, axis=1, keepdims=True)
    place_first = first * slots + rank_first.astype(jnp.int32)
    place_second = second * slots + rank_second.astype(jnp.int32)
    place_ref[:, 0:1] = place_first
    place_ref[:, 1:2] = place_second
    spots = lax.broadcasted_iota(jnp.int32, (count, places), 1)
    chosen = ((spots == place_first) | (spots == place_second)).astype(F32)
    send = jnp.dot(chosen.T.astype(BF16), normed, preferred_element_type=F32)
    send_ref[...] = send.astype(BF16)


def dispatch(tokens, routes, places, slots):
    return pl.pallas_call(
        functools.partial(dispatch_kernel, slots),
        out_shape=[
            jax.ShapeDtypeStruct((places, tokens.shape[1]), BF16),
            jax.ShapeDtypeStruct(routes.shape, jnp.int32),
        ],
        compiler_params=pltpu.CompilerParams(vmem_limit_bytes=16 * 2**20),
    )(tokens, routes)


def combine_kernel(
    lengths_ref, returned_ref, tokens_ref, place_ref, gates_ref, gain_ref, embed_ref, copies_ref
):
    count = tokens_ref.shape[0]
    captions = embed_ref.shape[0]
    returned = returned_ref[...]
    spots = lax.broadcasted_iota(jnp.int32, (count, returned.shape[0]), 1)
    gates = jnp.where(spots == place_ref[:, 0:1], gates_ref[:, 0:1], 0.0) + jnp.where(
        spots == place_ref[:, 1:2], gates_ref[:, 1:2], 0.0
    )
    high, low = split_pair(gates)
    mixed = tokens_ref[...].astype(F32)
    mixed += jnp.dot(high, returned, preferred_element_type=F32)
    mixed += jnp.dot(low, returned, preferred_element_type=F32)
    final = layer_norm(mixed) * gain_ref[...]
    padded = 8
    caption = lax.broadcasted_iota(jnp.int32, (padded, count), 0)
    token = lax.broadcasted_iota(jnp.int32, (padded, count), 1)
    row = lax.broadcasted_iota(jnp.int32, (padded, 1), 0)
    inside = jnp.zeros((padded, count), F32)
    sizes = jnp.ones((padded, 1), F32)
    start = jnp.int32(0)
    for index in range(captions):
        size = lengths_ref[0, index]
        here = (caption == index) & (token >= start) & (token < start + size)
        inside = jnp.where(here, 1.0, inside)
        sizes = jnp.where(row == index, size.astype(F32), sizes)
        start = start + size
    inside = inside.astype(BF16)
    first, rest = final.astype(BF16), final
    pooled = jnp.dot(inside, first, preferred_element_type=F32)
    for _ in range(2):
        rest = rest - first.astype(F32)
        first = rest.astype(BF16)
        pooled += jnp.dot(inside, first, preferred_element_type=F32)
    embed = unit_rows(pooled / sizes)[:captions]
    embed_ref[...] = embed
    unit = (embed * (1.0 / math.sqrt(embed.shape[1]))).astype(BF16)
    copies_ref[...] = jnp.broadcast_to(unit[None], copies_ref.shape)


def combine(lengths, returned, tokens, place, gates, gain, copies):
    captions = lengths.shape[1]
    width = tokens.shape[1]
    vmem = pl.BlockSpec(memory_space=pltpu.VMEM)
    return pl.pallas_call(
        combine_kernel,
        in_specs=[pl.BlockSpec(memory_space=pltpu.SMEM)] + [vmem] * 5,
        out_specs=[vmem, vmem],
        out_shape=[
            jax.ShapeDtypeStruct((captions, width), F32),
            jax.ShapeDtypeStruct((copies, captions, width), BF16),
        ],
        compiler_params=pltpu.CompilerParams(vmem_limit_bytes=24 * 2**20),
    )(lengths, returned, tokens, place, gates, gain.reshape(1, width))


def spread_kernel(*refs):
    rows_ref, copies_ref = refs[-2:]
    rows = jnp.concatenate([ref[...].astype(F32) for ref in refs[:-2]], axis=0).astype(BF16)
    rows_ref[...] = rows
    copies_ref[...] = jnp.broadcast_to(rows[None], copies_ref.shape)


def spread(parts, copies):
    count = sum(part.shape[0] for part in parts)
    width = parts[0].shape[1]
    return pl.pallas_call(
        spread_kernel,
        out_shape=[
            jax.ShapeDtypeStruct((count, width), BF16),
            jax.ShapeDtypeStruct((copies, count, width), BF16),
        ],
        compiler_params=pltpu.CompilerParams(vmem_limit_bytes=8 * 2**20),
    )(*parts)


def split_pair(values):
    high = values.astype(BF16)
    return high, (values - high.astype(F32)).astype(BF16)


def pair_slope(logits, same):
    signs = jnp.where(same, 1.0, -1.0).astype(F32)
    return -signs * jax.nn.sigmoid(-signs * logits)


def weighted_sum(coeff, rows):
    high, low = split_pair(coeff)
    both = jnp.dot(jnp.concatenate([high, low], axis=0), rows, preferred_element_type=F32)
    count = coeff.shape[0]
    return SIMILARITY_HEAT * (both[:count] + both[count:])


def held(*values):
    return lax.optimization_barrier(values)


def moved(values, target, mesh_shape):
    wide, deep, cores = mesh_shape
    pairs = []
    for index in range(wide * deep * cores):
        y, z, core = index // (deep * cores), index // cores % deep, index % cores
        y, z, core = target(y, z, core)
        pairs.append((index, (y % wide * deep + z % deep) * cores + core % cores))
    return lax.ppermute(values, "expert", pairs)


def along_expert(copies, shape):
    wide, deep, cores = shape
    chips = wide * deep
    groups = [[chip * cores + core for chip in range(chips)] for core in range(cores)]
    column = lax.all_to_all(
        copies, "expert", split_axis=0, concat_axis=0, axis_index_groups=groups, tiled=True
    ).reshape(chips * copies.shape[1], copies.shape[2])
    return on_chip(column, shape)


def on_chip(group, shape):
    return jnp.concatenate([group, moved(group, lambda y, z, c: (y, z, c + 1), shape)], axis=0)


def ring_shift(values, step, size):
    return lax.ppermute(values, "grid", [(i, (i + step) % size) for i in range(size)])


def unit_rows(values):
    return values * lax.rsqrt(jnp.mean(values * values, axis=-1, keepdims=True) + EPSILON)


def on_device(
    tokens, routes, route_gates, caption_lengths, image_embed, final_gain, up_weight, down_weight
):
    token_count, width = tokens.shape
    experts_all = lax.axis_size("expert")
    grid_all = lax.axis_size("grid")
    slots = 4 * token_count // experts_all
    places_all = experts_all * slots
    scale_root = math.sqrt(width)

    picture_unit = (unit_rows(image_embed.astype(F32)) / scale_root).astype(BF16)
    captions_here = picture_unit.shape[0]
    shape = (grid_all, experts_all // (2 * grid_all), 2)
    chip = lax.axis_index("expert") // shape[2]

    row_parts = [picture_unit] + [ring_shift(picture_unit, k, grid_all) for k in range(1, grid_all)]
    send, place = dispatch(tokens, routes, places_all, slots)
    send = send.reshape(experts_all, slots, width)
    arrived = lax.all_to_all(send, "expert", split_axis=0, concat_axis=0, tiled=True)
    chips = shape[0] * shape[1]
    pictures_row, picture_copies = spread(row_parts, chips)
    arrived, picture_copies, pictures_row = held(arrived, picture_copies, pictures_row)
    rows = arrived.reshape(places_all, width)

    up_local = up_weight[0]
    down_local = down_weight[0]
    half = places_all // 2
    top, bottom = rows[:half], rows[half:]
    left_top = ring_shift(top, 1, grid_all)
    right_bottom = ring_shift(bottom, -1, grid_all)
    pictures_all = along_expert(picture_copies, shape)
    left_bottom = ring_shift(bottom, 1, grid_all)
    right_top = ring_shift(top, -1, grid_all)
    own_term = expert_part([rows], up_local, down_local)[0]
    own_term, left_top, right_bottom = held(own_term, left_top, right_bottom)
    far_top = ring_shift(left_top, 1, grid_all)
    far_bottom = ring_shift(right_bottom, -1, grid_all)
    left_top, right_bottom = expert_part([left_top, right_bottom], up_local, down_local)
    home_top = ring_shift(left_top, -1, grid_all)
    home_bottom = ring_shift(right_bottom, 1, grid_all)
    right_top, left_bottom, left_top, right_bottom = held(
        right_top, left_bottom, left_top, right_bottom
    )
    right_top, left_bottom = expert_part([right_top, left_bottom], up_local, down_local)
    far_top, far_bottom, left_top, right_bottom, right_top, left_bottom = held(
        far_top, far_bottom, left_top, right_bottom, right_top, left_bottom
    )
    far_top, far_bottom = expert_part([far_top, far_bottom], up_local, down_local)
    far_from_left = ring_shift(far_top, 1, grid_all)
    far_from_right = ring_shift(far_bottom, -1, grid_all)
    far_from_left, far_from_right, home_top, home_bottom, pictures_all = held(
        far_from_left, far_from_right, home_top, home_bottom, pictures_all
    )
    right_top = (right_top.astype(F32) + far_from_left.astype(F32)).astype(BF16)
    left_bottom = (left_bottom.astype(F32) + far_from_right.astype(F32)).astype(BF16)
    last_top = ring_shift(right_top, 1, grid_all)
    last_bottom = ring_shift(left_bottom, -1, grid_all)
    total = sum_terms(own_term, home_top, last_top, home_bottom, last_bottom)
    results = total.reshape(experts_all, slots, width)
    returned = lax.all_to_all(results, "expert", split_axis=0, concat_axis=0, tiled=True)
    returned = returned.reshape(places_all, width)

    text_embed, text_copies = combine(
        caption_lengths, returned, tokens, place, route_gates, final_gain, chips
    )
    text_unit = text_copies[0]
    text_column = along_expert(text_copies, shape)

    def slopes(mine, others, place):
        logits = SIMILARITY_HEAT * lax.dot_general(
            mine, others, (((1,), (1,)), ((), ())), preferred_element_type=F32
        )
        row_ids = lax.broadcasted_iota(jnp.int32, logits.shape, 0)
        column_ids = lax.broadcasted_iota(jnp.int32, logits.shape, 1)
        same = (row_ids < captions_here) & (row_ids + place == column_ids)
        return weighted_sum(pair_slope(logits, same), others)

    sentence_slope = slopes(text_unit, pictures_all, chip * pictures_row.shape[0])
    partial = slopes(pictures_row, text_column, chip * captions_here).reshape(grid_all, captions_here, width)
    picture_slope = partial[0]
    for k in range(1, grid_all):
        picture_slope = picture_slope + ring_shift(partial[k], -k, grid_all)
    return (text_embed, sentence_slope, picture_slope)


def solution(mesh):
    split = P(("expert", "grid"), None)
    weights = P("expert", None, "grid")

    return jax.shard_map(
        on_device,
        mesh=mesh,
        in_specs=(split, split, split, split, split, P(), weights, weights),
        out_specs=(split, split, split),
        check_vma=False,
    )
```

```python
import functools
import math

import jax
import jax.numpy as jnp
from jax import lax
from jax.experimental import pallas as pl
from jax.experimental.pallas import tpu as pltpu
from jax.sharding import PartitionSpec as P

EPSILON = 1e-06
SIMILARITY_HEAT = 10.0
BF16 = jnp.bfloat16
F32 = jnp.float32


def layer_norm(values):
    centred = values - jnp.mean(values, axis=-1, keepdims=True)
    return centred * lax.rsqrt(jnp.mean(centred * centred, axis=-1, keepdims=True) + EPSILON)


def expert_kernel(*refs):
    blocks = (len(refs) - 3) // 2
    rows_refs, (up_ref, down_ref) = refs[:blocks], refs[blocks : blocks + 2]
    out_refs, hidden_ref = refs[blocks + 2 : -1], refs[-1]
    step = pl.program_id(0)
    half = pl.num_programs(0) // 2
    tile = up_ref.shape[1]

    @pl.when(step < half)
    def _():
        rows = jnp.concatenate([ref[...] for ref in rows_refs], axis=0)
        hidden = jnp.dot(rows, up_ref[...], preferred_element_type=F32)
        hidden = (0.5 * hidden * (1.0 + lax.erf(hidden * math.sqrt(0.5)))).astype(BF16)
        hidden_ref[:, pl.ds(pl.multiple_of(step * tile, tile), tile)] = hidden

    @pl.when(step >= half)
    def _():
        term = lax.dot_general(
            hidden_ref[...], down_ref[...], (((1,), (1,)), ((), ())), preferred_element_type=F32
        ).astype(BF16)
        start = 0
        for ref in out_refs:
            ref[...] = term[start : start + ref.shape[0]]
            start += ref.shape[0]


def expert_part(blocks, up_piece, down_piece):
    width, units = up_piece.shape
    count = sum(block.shape[0] for block in blocks)
    tile = min(512, units)
    half = units // tile
    return pl.pallas_call(
        expert_kernel,
        grid=(2 * half,),
        in_specs=[pl.BlockSpec(block.shape, lambda i: (0, 0)) for block in blocks]
        + [
            pl.BlockSpec((width, tile), lambda i: (0, jnp.minimum(i, half - 1))),
            pl.BlockSpec((width // half, units), lambda i: (jnp.maximum(i - half, 0), 0)),
        ],
        out_specs=[
            pl.BlockSpec((block.shape[0], width // half), lambda i: (0, jnp.maximum(i - half, 0)))
            for block in blocks
        ],
        out_shape=[jax.ShapeDtypeStruct(block.shape, BF16) for block in blocks],
        scratch_shapes=[pltpu.VMEM((count, units), BF16)],
        compiler_params=pltpu.CompilerParams(vmem_limit_bytes=63 * 2**20),
        cost_estimate=pl.CostEstimate(
            flops=12 * count * width * units,
            bytes_accessed=4 * width * units + 4 * count * width,
            transcendentals=count * units,
        ),
    )(*blocks, up_piece, down_piece)


def sum_kernel(own_ref, home_top, last_top, home_bottom, last_bottom, out_ref):
    own = own_ref[...].astype(F32)
    early = pl.program_id(0) < pl.num_programs(0) // 2

    @pl.when(early)
    def _():
        out_ref[...] = (own + home_top[...].astype(F32) + last_top[...].astype(F32)).astype(BF16)

    @pl.when(jnp.logical_not(early))
    def _():
        out_ref[...] = (
            own + home_bottom[...].astype(F32) + last_bottom[...].astype(F32)
        ).astype(BF16)


def sum_terms(own, home_top, last_top, home_bottom, last_bottom):
    count, width = own.shape
    steps = 4
    block = (count // steps, width)
    top = pl.BlockSpec(block, lambda i: (jnp.minimum(i, steps // 2 - 1), 0))
    bottom = pl.BlockSpec(block, lambda i: (jnp.maximum(i - steps // 2, 0), 0))
    return pl.pallas_call(
        sum_kernel,
        grid=(steps,),
        in_specs=[pl.BlockSpec(block, lambda i: (i, 0)), top, top, bottom, bottom],
        out_specs=pl.BlockSpec(block, lambda i: (i, 0)),
        out_shape=jax.ShapeDtypeStruct(own.shape, BF16),
        compiler_params=pltpu.CompilerParams(vmem_limit_bytes=16 * 2**20),
    )(own, home_top, last_top, home_bottom, last_bottom)


def dispatch_kernel(slots, tokens_ref, routes_ref, send_ref, place_ref, normed_ref):
    count = tokens_ref.shape[0]
    rows = send_ref.shape[0]
    step = pl.program_id(0)

    @pl.when(step == 0)
    def _():
        normed_ref[...] = layer_norm(tokens_ref[...].astype(F32)).astype(BF16)
        first, second = routes_ref[0:1, :], routes_ref[1:2, :]
        experts = rows * pl.num_programs(0) // slots
        names = lax.broadcasted_iota(jnp.int32, (experts, count), 0)
        hot_first = (first == names).astype(F32)
        hot_second = (second == names).astype(F32)
        column_ids = lax.broadcasted_iota(jnp.int32, (count, count), 1)
        row_ids = lax.broadcasted_iota(jnp.int32, (count, count), 0)
        before = (row_ids < column_ids).astype(F32).astype(BF16)
        rank_first = jnp.dot(hot_first.astype(BF16), before, preferred_element_type=F32)
        rank_second = jnp.dot(hot_second.astype(BF16), before, preferred_element_type=F32)
        rank_second = rank_second + jnp.sum(hot_first, axis=1, keepdims=True)
        rank_first = jnp.sum(rank_first * hot_first, axis=0, keepdims=True)
        rank_second = jnp.sum(rank_second * hot_second, axis=0, keepdims=True)
        place_ref[0:1, :] = first * slots + rank_first.astype(jnp.int32)
        place_ref[1:2, :] = second * slots + rank_second.astype(jnp.int32)

    spots = lax.broadcasted_iota(jnp.int32, (rows, count), 0) + step * rows
    chosen = ((spots == place_ref[0:1, :]) | (spots == place_ref[1:2, :])).astype(F32)
    send = jnp.dot(chosen.astype(BF16), normed_ref[...], preferred_element_type=F32)
    send_ref[...] = send.astype(BF16)


def dispatch(tokens, routes, places, slots):
    steps = 4
    count, width = tokens.shape
    return pl.pallas_call(
        functools.partial(dispatch_kernel, slots),
        grid=(steps,),
        in_specs=[
            pl.BlockSpec(tokens.shape, lambda i: (0, 0)),
            pl.BlockSpec(routes.shape, lambda i: (0, 0)),
        ],
        out_specs=[
            pl.BlockSpec((places // steps, width), lambda i: (i, 0)),
            pl.BlockSpec(routes.shape, lambda i: (0, 0)),
        ],
        out_shape=[
            jax.ShapeDtypeStruct((places, width), BF16),
            jax.ShapeDtypeStruct(routes.shape, jnp.int32),
        ],
        scratch_shapes=[pltpu.VMEM((count, width), BF16)],
        compiler_params=pltpu.CompilerParams(vmem_limit_bytes=63 * 2**20),
    )(tokens, routes)


def combine_kernel(
    lengths_ref, returned_ref, tokens_ref, place_ref, gates_ref, gain_ref, embed_ref, copies_ref
):
    count = tokens_ref.shape[0]
    captions = embed_ref.shape[0]
    returned = returned_ref[...]
    spots = lax.broadcasted_iota(jnp.int32, (count, returned.shape[0]), 1)
    zeros = jnp.zeros((4, count), F32)
    columns = jnp.concatenate([place_ref[...].astype(F32), gates_ref[...], zeros], axis=0).T
    places = columns[:, 0:2].astype(jnp.int32)
    gates = jnp.where(spots == places[:, 0:1], columns[:, 2:3], 0.0) + jnp.where(
        spots == places[:, 1:2], columns[:, 3:4], 0.0
    )
    high, low = split_pair(gates)
    mixed = tokens_ref[...].astype(F32)
    mixed += jnp.dot(high, returned, preferred_element_type=F32)
    mixed += jnp.dot(low, returned, preferred_element_type=F32)
    final = layer_norm(mixed) * gain_ref[...]
    padded = 8
    caption = lax.broadcasted_iota(jnp.int32, (padded, count), 0)
    token = lax.broadcasted_iota(jnp.int32, (padded, count), 1)
    row = lax.broadcasted_iota(jnp.int32, (padded, 1), 0)
    inside = jnp.zeros((padded, count), F32)
    sizes = jnp.ones((padded, 1), F32)
    start = jnp.int32(0)
    for index in range(captions):
        size = lengths_ref[0, index]
        here = (caption == index) & (token >= start) & (token < start + size)
        inside = jnp.where(here, 1.0, inside)
        sizes = jnp.where(row == index, size.astype(F32), sizes)
        start = start + size
    inside = inside.astype(BF16)
    first, rest = final.astype(BF16), final
    pooled = jnp.dot(inside, first, preferred_element_type=F32)
    for _ in range(2):
        rest = rest - first.astype(F32)
        first = rest.astype(BF16)
        pooled += jnp.dot(inside, first, preferred_element_type=F32)
    embed = unit_rows(pooled / sizes)[:captions]
    embed_ref[...] = embed
    unit = (embed * (1.0 / math.sqrt(embed.shape[1]))).astype(BF16)
    copies_ref[...] = jnp.broadcast_to(unit[None], copies_ref.shape)


def combine(lengths, returned, tokens, place, gates, gain, copies):
    captions = lengths.shape[1]
    width = tokens.shape[1]
    vmem = pl.BlockSpec(memory_space=pltpu.VMEM)
    return pl.pallas_call(
        combine_kernel,
        in_specs=[pl.BlockSpec(memory_space=pltpu.SMEM)] + [vmem] * 5,
        out_specs=[vmem, vmem],
        out_shape=[
            jax.ShapeDtypeStruct((captions, width), F32),
            jax.ShapeDtypeStruct((copies, captions, width), BF16),
        ],
        compiler_params=pltpu.CompilerParams(vmem_limit_bytes=24 * 2**20),
    )(lengths, returned, tokens, place, gates, gain.reshape(1, width))


def spread_kernel(*refs):
    rows_ref, copies_ref = refs[-2:]
    rows = jnp.concatenate([ref[...].astype(F32) for ref in refs[:-2]], axis=0).astype(BF16)
    rows_ref[...] = rows
    copies_ref[...] = jnp.broadcast_to(rows[None], copies_ref.shape)


def spread(parts, copies):
    count = sum(part.shape[0] for part in parts)
    width = parts[0].shape[1]
    return pl.pallas_call(
        spread_kernel,
        out_shape=[
            jax.ShapeDtypeStruct((count, width), BF16),
            jax.ShapeDtypeStruct((copies, count, width), BF16),
        ],
        compiler_params=pltpu.CompilerParams(vmem_limit_bytes=8 * 2**20),
    )(*parts)


def split_pair(values):
    high = values.astype(BF16)
    return high, (values - high.astype(F32)).astype(BF16)


def pair_slope(logits, same):
    signs = jnp.where(same, 1.0, -1.0).astype(F32)
    return -signs * jax.nn.sigmoid(-signs * logits)


def weighted_sum(coeff, rows):
    high, low = split_pair(coeff)
    both = jnp.dot(jnp.concatenate([high, low], axis=0), rows, preferred_element_type=F32)
    count = coeff.shape[0]
    return SIMILARITY_HEAT * (both[:count] + both[count:])


def held(*values):
    return lax.optimization_barrier(values)


def moved(values, target, mesh_shape):
    wide, deep, cores = mesh_shape
    pairs = []
    for index in range(wide * deep * cores):
        y, z, core = index // (deep * cores), index // cores % deep, index % cores
        y, z, core = target(y, z, core)
        pairs.append((index, (y % wide * deep + z % deep) * cores + core % cores))
    return lax.ppermute(values, "expert", pairs)


def along_expert(copies, shape):
    wide, deep, cores = shape
    chips = wide * deep
    groups = [[chip * cores + core for chip in range(chips)] for core in range(cores)]
    column = lax.all_to_all(
        copies, "expert", split_axis=0, concat_axis=0, axis_index_groups=groups, tiled=True
    ).reshape(chips * copies.shape[1], copies.shape[2])
    return on_chip(column, shape)


def on_chip(group, shape):
    return jnp.concatenate([group, moved(group, lambda y, z, c: (y, z, c + 1), shape)], axis=0)


def ring_shift(values, step, size):
    return lax.ppermute(values, "grid", [(i, (i + step) % size) for i in range(size)])


def unit_rows(values):
    return values * lax.rsqrt(jnp.mean(values * values, axis=-1, keepdims=True) + EPSILON)


def on_device(
    tokens, routes, route_gates, caption_lengths, image_embed, final_gain, up_weight, down_weight
):
    token_count, width = tokens.shape
    experts_all = lax.axis_size("expert")
    grid_all = lax.axis_size("grid")
    slots = 4 * token_count // experts_all
    places_all = experts_all * slots
    scale_root = math.sqrt(width)

    picture_unit = (unit_rows(image_embed.astype(F32)) / scale_root).astype(BF16)
    captions_here = picture_unit.shape[0]
    shape = (grid_all, experts_all // (2 * grid_all), 2)
    chip = lax.axis_index("expert") // shape[2]

    row_parts = [picture_unit] + [ring_shift(picture_unit, k, grid_all) for k in range(1, grid_all)]
    send, place = dispatch(tokens, routes.T, places_all, slots)
    send = send.reshape(experts_all, slots, width)
    arrived = lax.all_to_all(send, "expert", split_axis=0, concat_axis=0, tiled=True)
    chips = shape[0] * shape[1]
    pictures_row, picture_copies = spread(row_parts, chips)
    arrived, picture_copies, pictures_row = held(arrived, picture_copies, pictures_row)
    rows = arrived.reshape(places_all, width)

    up_local = up_weight[0]
    down_local = down_weight[0]
    half = places_all // 2
    top, bottom = rows[:half], rows[half:]
    left_top = ring_shift(top, 1, grid_all)
    right_bottom = ring_shift(bottom, -1, grid_all)
    pictures_all = along_expert(picture_copies, shape)
    left_bottom = ring_shift(bottom, 1, grid_all)
    right_top = ring_shift(top, -1, grid_all)
    far_top = ring_shift(left_top, 1, grid_all)
    far_bottom = ring_shift(right_bottom, -1, grid_all)
    left_top, right_bottom = expert_part([left_top, right_bottom], up_local, down_local)
    home_top = ring_shift(left_top, -1, grid_all)
    home_bottom = ring_shift(right_bottom, 1, grid_all)
    right_top, left_bottom, left_top, right_bottom = held(
        right_top, left_bottom, left_top, right_bottom
    )
    right_top, left_bottom = expert_part([right_top, left_bottom], up_local, down_local)
    far_top, far_bottom, left_top, right_bottom, right_top, left_bottom = held(
        far_top, far_bottom, left_top, right_bottom, right_top, left_bottom
    )
    far_top, far_bottom = expert_part([far_top, far_bottom], up_local, down_local)
    rows, far_top, far_bottom = held(rows, far_top, far_bottom)
    own_term = expert_part([rows], up_local, down_local)[0]
    far_from_left = ring_shift(far_top, 1, grid_all)
    far_from_right = ring_shift(far_bottom, -1, grid_all)
    far_from_left, far_from_right, home_top, home_bottom, pictures_all, own_term = held(
        far_from_left, far_from_right, home_top, home_bottom, pictures_all, own_term
    )
    right_top = (right_top.astype(F32) + far_from_left.astype(F32)).astype(BF16)
    left_bottom = (left_bottom.astype(F32) + far_from_right.astype(F32)).astype(BF16)
    last_top = ring_shift(right_top, 1, grid_all)
    last_bottom = ring_shift(left_bottom, -1, grid_all)
    total = sum_terms(own_term, home_top, last_top, home_bottom, last_bottom)
    results = total.reshape(experts_all, slots, width)
    returned = lax.all_to_all(results, "expert", split_axis=0, concat_axis=0, tiled=True)
    returned = returned.reshape(places_all, width)

    text_embed, text_copies = combine(
        caption_lengths, returned, tokens, place, route_gates.T, final_gain, chips
    )
    text_unit = text_copies[0]
    text_column = along_expert(text_copies, shape)

    def slopes(mine, others, place):
        logits = SIMILARITY_HEAT * lax.dot_general(
            mine, others, (((1,), (1,)), ((), ())), preferred_element_type=F32
        )
        row_ids = lax.broadcasted_iota(jnp.int32, logits.shape, 0)
        column_ids = lax.broadcasted_iota(jnp.int32, logits.shape, 1)
        same = (row_ids < captions_here) & (row_ids + place == column_ids)
        return weighted_sum(pair_slope(logits, same), others)

    sentence_slope = slopes(text_unit, pictures_all, chip * pictures_row.shape[0])
    partial = slopes(pictures_row, text_column, chip * captions_here).reshape(grid_all, captions_here, width)
    picture_slope = partial[0]
    for k in range(1, grid_all):
        picture_slope = picture_slope + ring_shift(partial[k], -k, grid_all)
    return (text_embed, sentence_slope, picture_slope)


def solution(mesh):
    split = P(("expert", "grid"), None)
    weights = P("expert", None, "grid")

    return jax.shard_map(
        on_device,
        mesh=mesh,
        in_specs=(split, split, split, split, split, P(), weights, weights),
        out_specs=(split, split, split),
        check_vma=False,
    )
```

```python
import functools
import math

import jax
import jax.numpy as jnp
from jax import lax
from jax.experimental import pallas as pl
from jax.experimental.pallas import tpu as pltpu
from jax.sharding import PartitionSpec as P

EPSILON = 1e-06
SIMILARITY_HEAT = 10.0
BF16 = jnp.bfloat16
F32 = jnp.float32


def layer_norm(values):
    centred = values - jnp.mean(values, axis=-1, keepdims=True)
    return centred * lax.rsqrt(jnp.mean(centred * centred, axis=-1, keepdims=True) + EPSILON)


def expert_kernel(*refs):
    blocks = (len(refs) - 3) // 2
    rows_refs, (up_ref, down_ref) = refs[:blocks], refs[blocks : blocks + 2]
    out_refs, hidden_ref = refs[blocks + 2 : -1], refs[-1]
    step = pl.program_id(0)
    half = pl.num_programs(0) // 2
    tile = up_ref.shape[1]

    @pl.when(step < half)
    def _():
        rows = jnp.concatenate([ref[...] for ref in rows_refs], axis=0)
        hidden = jnp.dot(rows, up_ref[...], preferred_element_type=F32)
        hidden = (0.5 * hidden * (1.0 + lax.erf(hidden * math.sqrt(0.5)))).astype(BF16)
        hidden_ref[:, pl.ds(pl.multiple_of(step * tile, tile), tile)] = hidden

    @pl.when(step >= half)
    def _():
        term = lax.dot_general(
            hidden_ref[...], down_ref[...], (((1,), (1,)), ((), ())), preferred_element_type=F32
        ).astype(BF16)
        start = 0
        for ref in out_refs:
            ref[...] = term[start : start + ref.shape[0]]
            start += ref.shape[0]


def expert_part(blocks, up_piece, down_piece):
    width, units = up_piece.shape
    count = sum(block.shape[0] for block in blocks)
    tile = min(512, units)
    half = units // tile
    return pl.pallas_call(
        expert_kernel,
        grid=(2 * half,),
        in_specs=[pl.BlockSpec(block.shape, lambda i: (0, 0)) for block in blocks]
        + [
            pl.BlockSpec((width, tile), lambda i: (0, jnp.minimum(i, half - 1))),
            pl.BlockSpec((width // half, units), lambda i: (jnp.maximum(i - half, 0), 0)),
        ],
        out_specs=[
            pl.BlockSpec((block.shape[0], width // half), lambda i: (0, jnp.maximum(i - half, 0)))
            for block in blocks
        ],
        out_shape=[jax.ShapeDtypeStruct(block.shape, BF16) for block in blocks],
        scratch_shapes=[pltpu.VMEM((count, units), BF16)],
        compiler_params=pltpu.CompilerParams(vmem_limit_bytes=12 * 2**20),
        cost_estimate=pl.CostEstimate(
            flops=12 * count * width * units,
            bytes_accessed=4 * width * units + 4 * count * width,
            transcendentals=count * units,
        ),
    )(*blocks, up_piece, down_piece)


def sum_kernel(own_ref, home_top, last_top, home_bottom, last_bottom, out_ref):
    own = own_ref[...].astype(F32)
    early = pl.program_id(0) < pl.num_programs(0) // 2

    @pl.when(early)
    def _():
        out_ref[...] = (own + home_top[...].astype(F32) + last_top[...].astype(F32)).astype(BF16)

    @pl.when(jnp.logical_not(early))
    def _():
        out_ref[...] = (
            own + home_bottom[...].astype(F32) + last_bottom[...].astype(F32)
        ).astype(BF16)


def sum_terms(own, home_top, last_top, home_bottom, last_bottom):
    count, width = own.shape
    steps = 4
    block = (count // steps, width)
    top = pl.BlockSpec(block, lambda i: (jnp.minimum(i, steps // 2 - 1), 0))
    bottom = pl.BlockSpec(block, lambda i: (jnp.maximum(i - steps // 2, 0), 0))
    return pl.pallas_call(
        sum_kernel,
        grid=(steps,),
        in_specs=[pl.BlockSpec(block, lambda i: (i, 0)), top, top, bottom, bottom],
        out_specs=pl.BlockSpec(block, lambda i: (i, 0)),
        out_shape=jax.ShapeDtypeStruct(own.shape, BF16),
        compiler_params=pltpu.CompilerParams(vmem_limit_bytes=12 * 2**20),
    )(own, home_top, last_top, home_bottom, last_bottom)


def dispatch_kernel(slots, tokens_ref, routes_ref, send_ref, place_ref, normed_ref):
    count = tokens_ref.shape[0]
    rows = send_ref.shape[0]
    step = pl.program_id(0)

    @pl.when(step == 0)
    def _():
        normed_ref[...] = layer_norm(tokens_ref[...].astype(F32)).astype(BF16)
        first, second = routes_ref[0:1, :], routes_ref[1:2, :]
        experts = rows * pl.num_programs(0) // slots
        names = lax.broadcasted_iota(jnp.int32, (experts, count), 0)
        hot_first = (first == names).astype(F32)
        hot_second = (second == names).astype(F32)
        column_ids = lax.broadcasted_iota(jnp.int32, (count, count), 1)
        row_ids = lax.broadcasted_iota(jnp.int32, (count, count), 0)
        before = (row_ids < column_ids).astype(F32).astype(BF16)
        rank_first = jnp.dot(hot_first.astype(BF16), before, preferred_element_type=F32)
        rank_second = jnp.dot(hot_second.astype(BF16), before, preferred_element_type=F32)
        rank_second = rank_second + jnp.sum(hot_first, axis=1, keepdims=True)
        rank_first = jnp.sum(rank_first * hot_first, axis=0, keepdims=True)
        rank_second = jnp.sum(rank_second * hot_second, axis=0, keepdims=True)
        place_ref[0:1, :] = first * slots + rank_first.astype(jnp.int32)
        place_ref[1:2, :] = second * slots + rank_second.astype(jnp.int32)

    spots = lax.broadcasted_iota(jnp.int32, (rows, count), 0) + step * rows
    chosen = ((spots == place_ref[0:1, :]) | (spots == place_ref[1:2, :])).astype(F32)
    send = jnp.dot(chosen.astype(BF16), normed_ref[...], preferred_element_type=F32)
    send_ref[...] = send.astype(BF16)


def dispatch(tokens, routes, places, slots):
    steps = 4
    count, width = tokens.shape
    return pl.pallas_call(
        functools.partial(dispatch_kernel, slots),
        grid=(steps,),
        in_specs=[
            pl.BlockSpec(tokens.shape, lambda i: (0, 0)),
            pl.BlockSpec(routes.shape, lambda i: (0, 0)),
        ],
        out_specs=[
            pl.BlockSpec((places // steps, width), lambda i: (i, 0)),
            pl.BlockSpec(routes.shape, lambda i: (0, 0)),
        ],
        out_shape=[
            jax.ShapeDtypeStruct((places, width), BF16),
            jax.ShapeDtypeStruct(routes.shape, jnp.int32),
        ],
        scratch_shapes=[pltpu.VMEM((count, width), BF16)],
        compiler_params=pltpu.CompilerParams(vmem_limit_bytes=12 * 2**20),
    )(tokens, routes)


def combine_kernel(
    lengths_ref, returned_ref, tokens_ref, place_ref, gates_ref, gain_ref, embed_ref, copies_ref
):
    count = tokens_ref.shape[0]
    captions = embed_ref.shape[0]
    returned = returned_ref[...]
    spots = lax.broadcasted_iota(jnp.int32, (count, returned.shape[0]), 1)
    zeros = jnp.zeros((4, count), F32)
    columns = jnp.concatenate([place_ref[...].astype(F32), gates_ref[...], zeros], axis=0).T
    places = columns[:, 0:2].astype(jnp.int32)
    gates = jnp.where(spots == places[:, 0:1], columns[:, 2:3], 0.0) + jnp.where(
        spots == places[:, 1:2], columns[:, 3:4], 0.0
    )
    high, low = split_pair(gates)
    mixed = tokens_ref[...].astype(F32)
    mixed += jnp.dot(high, returned, preferred_element_type=F32)
    mixed += jnp.dot(low, returned, preferred_element_type=F32)
    final = layer_norm(mixed) * gain_ref[...]
    padded = 8
    caption = lax.broadcasted_iota(jnp.int32, (padded, count), 0)
    token = lax.broadcasted_iota(jnp.int32, (padded, count), 1)
    row = lax.broadcasted_iota(jnp.int32, (padded, 1), 0)
    inside = jnp.zeros((padded, count), F32)
    sizes = jnp.ones((padded, 1), F32)
    start = jnp.int32(0)
    for index in range(captions):
        size = lengths_ref[0, index]
        here = (caption == index) & (token >= start) & (token < start + size)
        inside = jnp.where(here, 1.0, inside)
        sizes = jnp.where(row == index, size.astype(F32), sizes)
        start = start + size
    inside = inside.astype(BF16)
    first, rest = final.astype(BF16), final
    pooled = jnp.dot(inside, first, preferred_element_type=F32)
    for _ in range(2):
        rest = rest - first.astype(F32)
        first = rest.astype(BF16)
        pooled += jnp.dot(inside, first, preferred_element_type=F32)
    embed = unit_rows(pooled / sizes)[:captions]
    embed_ref[...] = embed
    unit = (embed * (1.0 / math.sqrt(embed.shape[1]))).astype(BF16)
    copies_ref[...] = jnp.broadcast_to(unit[None], copies_ref.shape)


def combine(lengths, returned, tokens, place, gates, gain, copies):
    captions = lengths.shape[1]
    width = tokens.shape[1]
    vmem = pl.BlockSpec(memory_space=pltpu.VMEM)
    return pl.pallas_call(
        combine_kernel,
        in_specs=[pl.BlockSpec(memory_space=pltpu.SMEM)] + [vmem] * 5,
        out_specs=[vmem, vmem],
        out_shape=[
            jax.ShapeDtypeStruct((captions, width), F32),
            jax.ShapeDtypeStruct((copies, captions, width), BF16),
        ],
        compiler_params=pltpu.CompilerParams(vmem_limit_bytes=12 * 2**20),
    )(lengths, returned, tokens, place, gates, gain.reshape(1, width))


def spread_kernel(*refs):
    rows_ref, copies_ref = refs[-2:]
    rows = jnp.concatenate([ref[...].astype(F32) for ref in refs[:-2]], axis=0).astype(BF16)
    rows_ref[...] = rows
    copies_ref[...] = jnp.broadcast_to(rows[None], copies_ref.shape)


def spread(parts, copies):
    count = sum(part.shape[0] for part in parts)
    width = parts[0].shape[1]
    return pl.pallas_call(
        spread_kernel,
        out_shape=[
            jax.ShapeDtypeStruct((count, width), BF16),
            jax.ShapeDtypeStruct((copies, count, width), BF16),
        ],
        compiler_params=pltpu.CompilerParams(vmem_limit_bytes=8 * 2**20),
    )(*parts)


def split_pair(values):
    high = values.astype(BF16)
    return high, (values - high.astype(F32)).astype(BF16)


def pair_slope(logits, same):
    signs = jnp.where(same, 1.0, -1.0).astype(F32)
    return -signs * jax.nn.sigmoid(-signs * logits)


def weighted_sum(coeff, rows):
    high, low = split_pair(coeff)
    both = jnp.dot(jnp.concatenate([high, low], axis=0), rows, preferred_element_type=F32)
    count = coeff.shape[0]
    return SIMILARITY_HEAT * (both[:count] + both[count:])


def held(*values):
    return lax.optimization_barrier(values)


def moved(values, target, mesh_shape):
    wide, deep, cores = mesh_shape
    pairs = []
    for index in range(wide * deep * cores):
        y, z, core = index // (deep * cores), index // cores % deep, index % cores
        y, z, core = target(y, z, core)
        pairs.append((index, (y % wide * deep + z % deep) * cores + core % cores))
    return lax.ppermute(values, "expert", pairs)


def along_expert(copies, shape):
    wide, deep, cores = shape
    chips = wide * deep
    groups = [[chip * cores + core for chip in range(chips)] for core in range(cores)]
    column = lax.all_to_all(
        copies, "expert", split_axis=0, concat_axis=0, axis_index_groups=groups, tiled=True
    ).reshape(chips * copies.shape[1], copies.shape[2])
    return on_chip(column, shape)


def on_chip(group, shape):
    return jnp.concatenate([group, moved(group, lambda y, z, c: (y, z, c + 1), shape)], axis=0)


def ring_shift(values, step, size):
    return lax.ppermute(values, "grid", [(i, (i + step) % size) for i in range(size)])


def unit_rows(values):
    return values * lax.rsqrt(jnp.mean(values * values, axis=-1, keepdims=True) + EPSILON)


def on_device(
    tokens, routes, route_gates, caption_lengths, image_embed, final_gain, up_weight, down_weight
):
    token_count, width = tokens.shape
    experts_all = lax.axis_size("expert")
    grid_all = lax.axis_size("grid")
    slots = 4 * token_count // experts_all
    places_all = experts_all * slots
    scale_root = math.sqrt(width)

    picture_unit = (unit_rows(image_embed.astype(F32)) / scale_root).astype(BF16)
    captions_here = picture_unit.shape[0]
    shape = (grid_all, experts_all // (2 * grid_all), 2)
    chip = lax.axis_index("expert") // shape[2]

    row_parts = [picture_unit] + [ring_shift(picture_unit, k, grid_all) for k in range(1, grid_all)]
    send, place = dispatch(tokens, routes.T, places_all, slots)
    send = send.reshape(experts_all, slots, width)
    arrived = lax.all_to_all(send, "expert", split_axis=0, concat_axis=0, tiled=True)
    chips = shape[0] * shape[1]
    pictures_row, picture_copies = spread(row_parts, chips)
    arrived, picture_copies, pictures_row = held(arrived, picture_copies, pictures_row)
    rows = arrived.reshape(places_all, width)

    up_local = up_weight[0]
    down_local = down_weight[0]
    half = places_all // 2
    top, bottom = rows[:half], rows[half:]
    left_top = ring_shift(top, 1, grid_all)
    right_bottom = ring_shift(bottom, -1, grid_all)
    pictures_all = along_expert(picture_copies, shape)
    left_bottom = ring_shift(bottom, 1, grid_all)
    right_top = ring_shift(top, -1, grid_all)
    far_top = ring_shift(left_top, 1, grid_all)
    far_bottom = ring_shift(right_bottom, -1, grid_all)
    left_top, right_bottom = expert_part([left_top, right_bottom], up_local, down_local)
    home_top = ring_shift(left_top, -1, grid_all)
    home_bottom = ring_shift(right_bottom, 1, grid_all)
    right_top, left_bottom, left_top, right_bottom = held(
        right_top, left_bottom, left_top, right_bottom
    )
    right_top, left_bottom = expert_part([right_top, left_bottom], up_local, down_local)
    far_top, far_bottom, left_top, right_bottom, right_top, left_bottom = held(
        far_top, far_bottom, left_top, right_bottom, right_top, left_bottom
    )
    far_top, far_bottom = expert_part([far_top, far_bottom], up_local, down_local)
    rows, far_top, far_bottom = held(rows, far_top, far_bottom)
    own_term = expert_part([rows], up_local, down_local)[0]
    far_from_left = ring_shift(far_top, 1, grid_all)
    far_from_right = ring_shift(far_bottom, -1, grid_all)
    far_from_left, far_from_right, home_top, home_bottom, own_term = held(
        far_from_left, far_from_right, home_top, home_bottom, own_term
    )
    right_top = (right_top.astype(F32) + far_from_left.astype(F32)).astype(BF16)
    left_bottom = (left_bottom.astype(F32) + far_from_right.astype(F32)).astype(BF16)
    last_top = ring_shift(right_top, 1, grid_all)
    last_bottom = ring_shift(left_bottom, -1, grid_all)
    total = sum_terms(own_term, home_top, last_top, home_bottom, last_bottom)
    results = total.reshape(experts_all, slots, width)
    returned = lax.all_to_all(results, "expert", split_axis=0, concat_axis=0, tiled=True)
    returned, pictures_all = held(returned, pictures_all)
    returned = returned.reshape(places_all, width)

    text_embed, text_copies = combine(
        caption_lengths, returned, tokens, place, route_gates.T, final_gain, chips
    )
    text_unit = text_copies[0]
    text_column = along_expert(text_copies, shape)

    def slopes(mine, others, place):
        logits = SIMILARITY_HEAT * lax.dot_general(
            mine, others, (((1,), (1,)), ((), ())), preferred_element_type=F32
        )
        row_ids = lax.broadcasted_iota(jnp.int32, logits.shape, 0)
        column_ids = lax.broadcasted_iota(jnp.int32, logits.shape, 1)
        same = (row_ids < captions_here) & (row_ids + place == column_ids)
        return weighted_sum(pair_slope(logits, same), others)

    sentence_slope = slopes(text_unit, pictures_all, chip * pictures_row.shape[0])
    partial = slopes(pictures_row, text_column, chip * captions_here).reshape(grid_all, captions_here, width)
    picture_slope = partial[0]
    for k in range(1, grid_all):
        picture_slope = picture_slope + ring_shift(partial[k], -k, grid_all)
    return (text_embed, sentence_slope, picture_slope)


def solution(mesh):
    split = P(("expert", "grid"), None)
    weights = P("expert", None, "grid")

    return jax.shard_map(
        on_device,
        mesh=mesh,
        in_specs=(split, split, split, split, split, P(), weights, weights),
        out_specs=(split, split, split),
        check_vma=False,
    )
```

```python
import functools
import math

import jax
import jax.numpy as jnp
from jax import lax
from jax.experimental import pallas as pl
from jax.experimental.pallas import tpu as pltpu
from jax.sharding import PartitionSpec as P

EPSILON = 1e-06
SIMILARITY_HEAT = 10.0
BF16 = jnp.bfloat16
F32 = jnp.float32


def layer_norm(values):
    centred = values - jnp.mean(values, axis=-1, keepdims=True)
    return centred * lax.rsqrt(jnp.mean(centred * centred, axis=-1, keepdims=True) + EPSILON)


def expert_kernel(*refs):
    blocks = (len(refs) - 3) // 2
    rows_refs, (up_ref, down_ref) = refs[:blocks], refs[blocks : blocks + 2]
    out_refs, hidden_ref = refs[blocks + 2 : -1], refs[-1]
    step = pl.program_id(0)
    half = pl.num_programs(0) // 2
    tile = up_ref.shape[1]

    @pl.when(step < half)
    def _():
        rows = jnp.concatenate([ref[...] for ref in rows_refs], axis=0)
        hidden = jnp.dot(rows, up_ref[...], preferred_element_type=F32)
        hidden = (0.5 * hidden * (1.0 + lax.erf(hidden * math.sqrt(0.5)))).astype(BF16)
        hidden_ref[:, pl.ds(pl.multiple_of(step * tile, tile), tile)] = hidden

    @pl.when(step >= half)
    def _():
        term = lax.dot_general(
            hidden_ref[...], down_ref[...], (((1,), (1,)), ((), ())), preferred_element_type=F32
        ).astype(BF16)
        start = 0
        for ref in out_refs:
            ref[...] = term[start : start + ref.shape[0]]
            start += ref.shape[0]


def expert_part(blocks, up_piece, down_piece):
    width, units = up_piece.shape
    count = sum(block.shape[0] for block in blocks)
    tile = min(512, units)
    half = units // tile
    return pl.pallas_call(
        expert_kernel,
        grid=(2 * half,),
        in_specs=[pl.BlockSpec(block.shape, lambda i: (0, 0)) for block in blocks]
        + [
            pl.BlockSpec((width, tile), lambda i: (0, jnp.minimum(i, half - 1))),
            pl.BlockSpec((width // half, units), lambda i: (jnp.maximum(i - half, 0), 0)),
        ],
        out_specs=[
            pl.BlockSpec((block.shape[0], width // half), lambda i: (0, jnp.maximum(i - half, 0)))
            for block in blocks
        ],
        out_shape=[jax.ShapeDtypeStruct(block.shape, BF16) for block in blocks],
        scratch_shapes=[pltpu.VMEM((count, units), BF16)],
        compiler_params=pltpu.CompilerParams(vmem_limit_bytes=12 * 2**20),
        cost_estimate=pl.CostEstimate(
            flops=12 * count * width * units,
            bytes_accessed=4 * width * units + 4 * count * width,
            transcendentals=count * units,
        ),
    )(*blocks, up_piece, down_piece)


def sum_kernel(own_ref, home_top, last_top, home_bottom, last_bottom, out_ref):
    own = own_ref[...].astype(F32)
    early = pl.program_id(0) < pl.num_programs(0) // 2

    @pl.when(early)
    def _():
        out_ref[...] = (own + home_top[...].astype(F32) + last_top[...].astype(F32)).astype(BF16)

    @pl.when(jnp.logical_not(early))
    def _():
        out_ref[...] = (
            own + home_bottom[...].astype(F32) + last_bottom[...].astype(F32)
        ).astype(BF16)


def sum_terms(own, home_top, last_top, home_bottom, last_bottom):
    count, width = own.shape
    steps = 4
    block = (count // steps, width)
    top = pl.BlockSpec(block, lambda i: (jnp.minimum(i, steps // 2 - 1), 0))
    bottom = pl.BlockSpec(block, lambda i: (jnp.maximum(i - steps // 2, 0), 0))
    return pl.pallas_call(
        sum_kernel,
        grid=(steps,),
        in_specs=[pl.BlockSpec(block, lambda i: (i, 0)), top, top, bottom, bottom],
        out_specs=pl.BlockSpec(block, lambda i: (i, 0)),
        out_shape=jax.ShapeDtypeStruct(own.shape, BF16),
        compiler_params=pltpu.CompilerParams(vmem_limit_bytes=12 * 2**20),
    )(own, home_top, last_top, home_bottom, last_bottom)


def dispatch_kernel(slots, tokens_ref, routes_ref, send_ref, place_ref, normed_ref):
    count = tokens_ref.shape[0]
    rows = send_ref.shape[0]
    step = pl.program_id(0)

    @pl.when(step == 0)
    def _():
        normed_ref[...] = layer_norm(tokens_ref[...].astype(F32)).astype(BF16)
        first, second = routes_ref[0:1, :], routes_ref[1:2, :]
        experts = rows * pl.num_programs(0) // slots
        names = lax.broadcasted_iota(jnp.int32, (experts, count), 0)
        hot_first = (first == names).astype(F32)
        hot_second = (second == names).astype(F32)
        column_ids = lax.broadcasted_iota(jnp.int32, (count, count), 1)
        row_ids = lax.broadcasted_iota(jnp.int32, (count, count), 0)
        before = (row_ids < column_ids).astype(F32).astype(BF16)
        rank_first = jnp.dot(hot_first.astype(BF16), before, preferred_element_type=F32)
        rank_second = jnp.dot(hot_second.astype(BF16), before, preferred_element_type=F32)
        rank_second = rank_second + jnp.sum(hot_first, axis=1, keepdims=True)
        rank_first = jnp.sum(rank_first * hot_first, axis=0, keepdims=True)
        rank_second = jnp.sum(rank_second * hot_second, axis=0, keepdims=True)
        place_ref[0:1, :] = first * slots + rank_first.astype(jnp.int32)
        place_ref[1:2, :] = second * slots + rank_second.astype(jnp.int32)

    spots = lax.broadcasted_iota(jnp.int32, (rows, count), 0) + step * rows
    chosen = ((spots == place_ref[0:1, :]) | (spots == place_ref[1:2, :])).astype(F32)
    send = jnp.dot(chosen.astype(BF16), normed_ref[...], preferred_element_type=F32)
    send_ref[...] = send.astype(BF16)


def dispatch(tokens, routes, places, slots):
    steps = 4
    count, width = tokens.shape
    return pl.pallas_call(
        functools.partial(dispatch_kernel, slots),
        grid=(steps,),
        in_specs=[
            pl.BlockSpec(tokens.shape, lambda i: (0, 0)),
            pl.BlockSpec(routes.shape, lambda i: (0, 0)),
        ],
        out_specs=[
            pl.BlockSpec((places // steps, width), lambda i: (i, 0)),
            pl.BlockSpec(routes.shape, lambda i: (0, 0)),
        ],
        out_shape=[
            jax.ShapeDtypeStruct((places, width), BF16),
            jax.ShapeDtypeStruct(routes.shape, jnp.int32),
        ],
        scratch_shapes=[pltpu.VMEM((count, width), BF16)],
        compiler_params=pltpu.CompilerParams(vmem_limit_bytes=63 * 2**20),
    )(tokens, routes)


def combine_kernel(
    lengths_ref, returned_ref, tokens_ref, place_ref, gates_ref, gain_ref, embed_ref, copies_ref
):
    count = tokens_ref.shape[0]
    captions = embed_ref.shape[0]
    returned = returned_ref[...]
    spots = lax.broadcasted_iota(jnp.int32, (count, returned.shape[0]), 1)
    zeros = jnp.zeros((4, count), F32)
    columns = jnp.concatenate([place_ref[...].astype(F32), gates_ref[...], zeros], axis=0).T
    places = columns[:, 0:2].astype(jnp.int32)
    gates = jnp.where(spots == places[:, 0:1], columns[:, 2:3], 0.0) + jnp.where(
        spots == places[:, 1:2], columns[:, 3:4], 0.0
    )
    high, low = split_pair(gates)
    mixed = tokens_ref[...].astype(F32)
    mixed += jnp.dot(high, returned, preferred_element_type=F32)
    mixed += jnp.dot(low, returned, preferred_element_type=F32)
    final = layer_norm(mixed) * gain_ref[...]
    padded = 8
    caption = lax.broadcasted_iota(jnp.int32, (padded, count), 0)
    token = lax.broadcasted_iota(jnp.int32, (padded, count), 1)
    row = lax.broadcasted_iota(jnp.int32, (padded, 1), 0)
    inside = jnp.zeros((padded, count), F32)
    sizes = jnp.ones((padded, 1), F32)
    start = jnp.int32(0)
    for index in range(captions):
        size = lengths_ref[0, index]
        here = (caption == index) & (token >= start) & (token < start + size)
        inside = jnp.where(here, 1.0, inside)
        sizes = jnp.where(row == index, size.astype(F32), sizes)
        start = start + size
    inside = inside.astype(BF16)
    first, rest = final.astype(BF16), final
    pooled = jnp.dot(inside, first, preferred_element_type=F32)
    for _ in range(2):
        rest = rest - first.astype(F32)
        first = rest.astype(BF16)
        pooled += jnp.dot(inside, first, preferred_element_type=F32)
    embed = unit_rows(pooled / sizes)[:captions]
    embed_ref[...] = embed
    unit = (embed * (1.0 / math.sqrt(embed.shape[1]))).astype(BF16)
    copies_ref[...] = jnp.broadcast_to(unit[None], copies_ref.shape)


def combine(lengths, returned, tokens, place, gates, gain, copies):
    captions = lengths.shape[1]
    width = tokens.shape[1]
    vmem = pl.BlockSpec(memory_space=pltpu.VMEM)
    return pl.pallas_call(
        combine_kernel,
        in_specs=[pl.BlockSpec(memory_space=pltpu.SMEM)] + [vmem] * 5,
        out_specs=[vmem, vmem],
        out_shape=[
            jax.ShapeDtypeStruct((captions, width), F32),
            jax.ShapeDtypeStruct((copies, captions, width), BF16),
        ],
        compiler_params=pltpu.CompilerParams(vmem_limit_bytes=12 * 2**20),
    )(lengths, returned, tokens, place, gates, gain.reshape(1, width))


def spread_kernel(*refs):
    rows_ref, copies_ref = refs[-2:]
    rows = jnp.concatenate([ref[...].astype(F32) for ref in refs[:-2]], axis=0).astype(BF16)
    rows_ref[...] = rows
    copies_ref[...] = jnp.broadcast_to(rows[None], copies_ref.shape)


def spread(parts, copies):
    count = sum(part.shape[0] for part in parts)
    width = parts[0].shape[1]
    return pl.pallas_call(
        spread_kernel,
        out_shape=[
            jax.ShapeDtypeStruct((count, width), BF16),
            jax.ShapeDtypeStruct((copies, count, width), BF16),
        ],
        compiler_params=pltpu.CompilerParams(vmem_limit_bytes=8 * 2**20),
    )(*parts)


def split_pair(values):
    high = values.astype(BF16)
    return high, (values - high.astype(F32)).astype(BF16)


def pair_slope(logits, same):
    signs = jnp.where(same, 1.0, -1.0).astype(F32)
    return -signs * jax.nn.sigmoid(-signs * logits)


def weighted_sum(coeff, rows):
    high, low = split_pair(coeff)
    both = jnp.dot(jnp.concatenate([high, low], axis=0), rows, preferred_element_type=F32)
    count = coeff.shape[0]
    return SIMILARITY_HEAT * (both[:count] + both[count:])


def held(*values):
    return lax.optimization_barrier(values)


def moved(values, target, mesh_shape):
    wide, deep, cores = mesh_shape
    pairs = []
    for index in range(wide * deep * cores):
        y, z, core = index // (deep * cores), index // cores % deep, index % cores
        y, z, core = target(y, z, core)
        pairs.append((index, (y % wide * deep + z % deep) * cores + core % cores))
    return lax.ppermute(values, "expert", pairs)


def along_expert(copies, shape):
    wide, deep, cores = shape
    chips = wide * deep
    groups = [[chip * cores + core for chip in range(chips)] for core in range(cores)]
    column = lax.all_to_all(
        copies, "expert", split_axis=0, concat_axis=0, axis_index_groups=groups, tiled=True
    ).reshape(chips * copies.shape[1], copies.shape[2])
    return on_chip(column, shape)


def on_chip(group, shape):
    return jnp.concatenate([group, moved(group, lambda y, z, c: (y, z, c + 1), shape)], axis=0)


def ring_shift(values, step, size):
    return lax.ppermute(values, "grid", [(i, (i + step) % size) for i in range(size)])


def unit_rows(values):
    return values * lax.rsqrt(jnp.mean(values * values, axis=-1, keepdims=True) + EPSILON)


def on_device(
    tokens, routes, route_gates, caption_lengths, image_embed, final_gain, up_weight, down_weight
):
    token_count, width = tokens.shape
    experts_all = lax.axis_size("expert")
    grid_all = lax.axis_size("grid")
    slots = 4 * token_count // experts_all
    places_all = experts_all * slots
    scale_root = math.sqrt(width)

    picture_unit = (unit_rows(image_embed.astype(F32)) / scale_root).astype(BF16)
    captions_here = picture_unit.shape[0]
    shape = (grid_all, experts_all // (2 * grid_all), 2)
    chip = lax.axis_index("expert") // shape[2]

    row_parts = [picture_unit] + [ring_shift(picture_unit, k, grid_all) for k in range(1, grid_all)]
    send, place = dispatch(tokens, routes.T, places_all, slots)
    send = send.reshape(experts_all, slots, width)
    arrived = lax.all_to_all(send, "expert", split_axis=0, concat_axis=0, tiled=True)
    chips = shape[0] * shape[1]
    pictures_row, picture_copies = spread(row_parts, chips)
    arrived, picture_copies, pictures_row = held(arrived, picture_copies, pictures_row)
    rows = arrived.reshape(places_all, width)

    up_local = up_weight[0]
    down_local = down_weight[0]
    half = places_all // 2
    top, bottom = rows[:half], rows[half:]
    left_top = ring_shift(top, 1, grid_all)
    right_bottom = ring_shift(bottom, -1, grid_all)
    pictures_all = along_expert(picture_copies, shape)
    left_bottom = ring_shift(bottom, 1, grid_all)
    right_top = ring_shift(top, -1, grid_all)
    own_term = expert_part([rows], up_local, down_local)[0]
    own_term, left_top, right_bottom = held(own_term, left_top, right_bottom)
    far_top = ring_shift(left_top, 1, grid_all)
    far_bottom = ring_shift(right_bottom, -1, grid_all)
    left_top, right_bottom = expert_part([left_top, right_bottom], up_local, down_local)
    home_top = ring_shift(left_top, -1, grid_all)
    home_bottom = ring_shift(right_bottom, 1, grid_all)
    right_top, left_bottom, left_top, right_bottom = held(
        right_top, left_bottom, left_top, right_bottom
    )
    right_top, left_bottom = expert_part([right_top, left_bottom], up_local, down_local)
    far_top, far_bottom, left_top, right_bottom, right_top, left_bottom = held(
        far_top, far_bottom, left_top, right_bottom, right_top, left_bottom
    )
    far_top, far_bottom = expert_part([far_top, far_bottom], up_local, down_local)
    far_from_left = ring_shift(far_top, 1, grid_all)
    far_from_right = ring_shift(far_bottom, -1, grid_all)
    far_from_left, far_from_right, home_top, home_bottom = held(
        far_from_left, far_from_right, home_top, home_bottom
    )
    right_top = (right_top.astype(F32) + far_from_left.astype(F32)).astype(BF16)
    left_bottom = (left_bottom.astype(F32) + far_from_right.astype(F32)).astype(BF16)
    last_top = ring_shift(right_top, 1, grid_all)
    last_bottom = ring_shift(left_bottom, -1, grid_all)
    total = sum_terms(own_term, home_top, last_top, home_bottom, last_bottom)
    results = total.reshape(experts_all, slots, width)
    returned = lax.all_to_all(results, "expert", split_axis=0, concat_axis=0, tiled=True)
    returned, pictures_all = held(returned, pictures_all)
    returned = returned.reshape(places_all, width)

    text_embed, text_copies = combine(
        caption_lengths, returned, tokens, place, route_gates.T, final_gain, chips
    )
    text_unit = text_copies[0]
    text_column = along_expert(text_copies, shape)

    def slopes(mine, others, place):
        logits = SIMILARITY_HEAT * lax.dot_general(
            mine, others, (((1,), (1,)), ((), ())), preferred_element_type=F32
        )
        row_ids = lax.broadcasted_iota(jnp.int32, logits.shape, 0)
        column_ids = lax.broadcasted_iota(jnp.int32, logits.shape, 1)
        same = (row_ids < captions_here) & (row_ids + place == column_ids)
        return weighted_sum(pair_slope(logits, same), others)

    sentence_slope = slopes(text_unit, pictures_all, chip * pictures_row.shape[0])
    partial = slopes(pictures_row, text_column, chip * captions_here).reshape(grid_all, captions_here, width)
    picture_slope = partial[0]
    for k in range(1, grid_all):
        picture_slope = picture_slope + ring_shift(partial[k], -k, grid_all)
    return (text_embed, sentence_slope, picture_slope)


def solution(mesh):
    split = P(("expert", "grid"), None)
    weights = P("expert", None, "grid")

    return jax.shard_map(
        on_device,
        mesh=mesh,
        in_specs=(split, split, split, split, split, P(), weights, weights),
        out_specs=(split, split, split),
        check_vma=False,
    )
```

```python
import functools
import math

import jax
import jax.numpy as jnp
from jax import lax
from jax.experimental import pallas as pl
from jax.experimental.pallas import tpu as pltpu
from jax.sharding import PartitionSpec as P

EPSILON = 1e-06
SIMILARITY_HEAT = 10.0
BF16 = jnp.bfloat16
F32 = jnp.float32


def layer_norm(values):
    centred = values - jnp.mean(values, axis=-1, keepdims=True)
    return centred * lax.rsqrt(jnp.mean(centred * centred, axis=-1, keepdims=True) + EPSILON)


def expert_kernel(*refs):
    blocks = (len(refs) - 3) // 2
    rows_refs, (up_ref, down_ref) = refs[:blocks], refs[blocks : blocks + 2]
    out_refs, hidden_ref = refs[blocks + 2 : -1], refs[-1]
    step = pl.program_id(0)
    half = pl.num_programs(0) // 2
    tile = up_ref.shape[1]

    @pl.when(step < half)
    def _():
        rows = jnp.concatenate([ref[...] for ref in rows_refs], axis=0)
        hidden = jnp.dot(rows, up_ref[...], preferred_element_type=F32)
        hidden = (0.5 * hidden * (1.0 + lax.erf(hidden * math.sqrt(0.5)))).astype(BF16)
        hidden_ref[:, pl.ds(pl.multiple_of(step * tile, tile), tile)] = hidden

    @pl.when(step >= half)
    def _():
        term = lax.dot_general(
            hidden_ref[...], down_ref[...], (((1,), (1,)), ((), ())), preferred_element_type=F32
        ).astype(BF16)
        start = 0
        for ref in out_refs:
            ref[...] = term[start : start + ref.shape[0]]
            start += ref.shape[0]


def expert_part(blocks, up_piece, down_piece):
    width, units = up_piece.shape
    count = sum(block.shape[0] for block in blocks)
    tile = min(512, units)
    half = units // tile
    return pl.pallas_call(
        expert_kernel,
        grid=(2 * half,),
        in_specs=[pl.BlockSpec(block.shape, lambda i: (0, 0)) for block in blocks]
        + [
            pl.BlockSpec((width, tile), lambda i: (0, jnp.minimum(i, half - 1))),
            pl.BlockSpec((width // half, units), lambda i: (jnp.maximum(i - half, 0), 0)),
        ],
        out_specs=[
            pl.BlockSpec((block.shape[0], width // half), lambda i: (0, jnp.maximum(i - half, 0)))
            for block in blocks
        ],
        out_shape=[jax.ShapeDtypeStruct(block.shape, BF16) for block in blocks],
        scratch_shapes=[pltpu.VMEM((count, units), BF16)],
        compiler_params=pltpu.CompilerParams(vmem_limit_bytes=56 * 2**20),
        cost_estimate=pl.CostEstimate(
            flops=12 * count * width * units,
            bytes_accessed=4 * width * units + 4 * count * width,
            transcendentals=count * units,
        ),
    )(*blocks, up_piece, down_piece)


def sum_kernel(own_ref, home_top, last_top, home_bottom, last_bottom, out_ref):
    own = own_ref[...].astype(F32)
    early = pl.program_id(0) < pl.num_programs(0) // 2

    @pl.when(early)
    def _():
        out_ref[...] = (own + home_top[...].astype(F32) + last_top[...].astype(F32)).astype(BF16)

    @pl.when(jnp.logical_not(early))
    def _():
        out_ref[...] = (
            own + home_bottom[...].astype(F32) + last_bottom[...].astype(F32)
        ).astype(BF16)


def sum_terms(own, home_top, last_top, home_bottom, last_bottom):
    count, width = own.shape
    steps = 4
    block = (count // steps, width)
    top = pl.BlockSpec(block, lambda i: (jnp.minimum(i, steps // 2 - 1), 0))
    bottom = pl.BlockSpec(block, lambda i: (jnp.maximum(i - steps // 2, 0), 0))
    return pl.pallas_call(
        sum_kernel,
        grid=(steps,),
        in_specs=[pl.BlockSpec(block, lambda i: (i, 0)), top, top, bottom, bottom],
        out_specs=pl.BlockSpec(block, lambda i: (i, 0)),
        out_shape=jax.ShapeDtypeStruct(own.shape, BF16),
        compiler_params=pltpu.CompilerParams(vmem_limit_bytes=16 * 2**20),
    )(own, home_top, last_top, home_bottom, last_bottom)


def dispatch_kernel(slots, tokens_ref, routes_ref, send_ref, place_ref, normed_ref):
    count = tokens_ref.shape[0]
    rows = send_ref.shape[0]
    step = pl.program_id(0)

    @pl.when(step == 0)
    def _():
        normed_ref[...] = layer_norm(tokens_ref[...].astype(F32)).astype(BF16)
        first, second = routes_ref[0:1, :], routes_ref[1:2, :]
        experts = rows * pl.num_programs(0) // slots
        names = lax.broadcasted_iota(jnp.int32, (experts, count), 0)
        hot_first = (first == names).astype(F32)
        hot_second = (second == names).astype(F32)
        column_ids = lax.broadcasted_iota(jnp.int32, (count, count), 1)
        row_ids = lax.broadcasted_iota(jnp.int32, (count, count), 0)
        before = (row_ids < column_ids).astype(F32).astype(BF16)
        rank_first = jnp.dot(hot_first.astype(BF16), before, preferred_element_type=F32)
        rank_second = jnp.dot(hot_second.astype(BF16), before, preferred_element_type=F32)
        rank_second = rank_second + jnp.sum(hot_first, axis=1, keepdims=True)
        rank_first = jnp.sum(rank_first * hot_first, axis=0, keepdims=True)
        rank_second = jnp.sum(rank_second * hot_second, axis=0, keepdims=True)
        place_ref[0:1, :] = first * slots + rank_first.astype(jnp.int32)
        place_ref[1:2, :] = second * slots + rank_second.astype(jnp.int32)

    spots = lax.broadcasted_iota(jnp.int32, (rows, count), 0) + step * rows
    chosen = ((spots == place_ref[0:1, :]) | (spots == place_ref[1:2, :])).astype(F32)
    send = jnp.dot(chosen.astype(BF16), normed_ref[...], preferred_element_type=F32)
    send_ref[...] = send.astype(BF16)


def dispatch(tokens, routes, places, slots):
    steps = 4
    count, width = tokens.shape
    return pl.pallas_call(
        functools.partial(dispatch_kernel, slots),
        grid=(steps,),
        in_specs=[
            pl.BlockSpec(tokens.shape, lambda i: (0, 0)),
            pl.BlockSpec(routes.shape, lambda i: (0, 0)),
        ],
        out_specs=[
            pl.BlockSpec((places // steps, width), lambda i: (i, 0)),
            pl.BlockSpec(routes.shape, lambda i: (0, 0)),
        ],
        out_shape=[
            jax.ShapeDtypeStruct((places, width), BF16),
            jax.ShapeDtypeStruct(routes.shape, jnp.int32),
        ],
        scratch_shapes=[pltpu.VMEM((count, width), BF16)],
        compiler_params=pltpu.CompilerParams(vmem_limit_bytes=63 * 2**20),
    )(tokens, routes)


def combine_kernel(
    lengths_ref, returned_ref, tokens_ref, place_ref, gates_ref, gain_ref, embed_ref, copies_ref
):
    count = tokens_ref.shape[0]
    captions = embed_ref.shape[0]
    returned = returned_ref[...]
    spots = lax.broadcasted_iota(jnp.int32, (count, returned.shape[0]), 1)
    zeros = jnp.zeros((4, count), F32)
    columns = jnp.concatenate([place_ref[...].astype(F32), gates_ref[...], zeros], axis=0).T
    places = columns[:, 0:2].astype(jnp.int32)
    gates = jnp.where(spots == places[:, 0:1], columns[:, 2:3], 0.0) + jnp.where(
        spots == places[:, 1:2], columns[:, 3:4], 0.0
    )
    high, low = split_pair(gates)
    mixed = tokens_ref[...].astype(F32)
    mixed += jnp.dot(high, returned, preferred_element_type=F32)
    mixed += jnp.dot(low, returned, preferred_element_type=F32)
    final = layer_norm(mixed) * gain_ref[...]
    padded = 8
    caption = lax.broadcasted_iota(jnp.int32, (padded, count), 0)
    token = lax.broadcasted_iota(jnp.int32, (padded, count), 1)
    row = lax.broadcasted_iota(jnp.int32, (padded, 1), 0)
    inside = jnp.zeros((padded, count), F32)
    sizes = jnp.ones((padded, 1), F32)
    start = jnp.int32(0)
    for index in range(captions):
        size = lengths_ref[0, index]
        here = (caption == index) & (token >= start) & (token < start + size)
        inside = jnp.where(here, 1.0, inside)
        sizes = jnp.where(row == index, size.astype(F32), sizes)
        start = start + size
    inside = inside.astype(BF16)
    first, rest = final.astype(BF16), final
    pooled = jnp.dot(inside, first, preferred_element_type=F32)
    for _ in range(2):
        rest = rest - first.astype(F32)
        first = rest.astype(BF16)
        pooled += jnp.dot(inside, first, preferred_element_type=F32)
    embed = unit_rows(pooled / sizes)[:captions]
    embed_ref[...] = embed
    unit = (embed * (1.0 / math.sqrt(embed.shape[1]))).astype(BF16)
    copies_ref[...] = jnp.broadcast_to(unit[None], copies_ref.shape)


def combine(lengths, returned, tokens, place, gates, gain, copies):
    captions = lengths.shape[1]
    width = tokens.shape[1]
    vmem = pl.BlockSpec(memory_space=pltpu.VMEM)
    return pl.pallas_call(
        combine_kernel,
        in_specs=[pl.BlockSpec(memory_space=pltpu.SMEM)] + [vmem] * 5,
        out_specs=[vmem, vmem],
        out_shape=[
            jax.ShapeDtypeStruct((captions, width), F32),
            jax.ShapeDtypeStruct((copies, captions, width), BF16),
        ],
        compiler_params=pltpu.CompilerParams(vmem_limit_bytes=24 * 2**20),
    )(lengths, returned, tokens, place, gates, gain.reshape(1, width))


def spread_kernel(*refs):
    rows_ref, copies_ref = refs[-2:]
    rows = jnp.concatenate([ref[...].astype(F32) for ref in refs[:-2]], axis=0).astype(BF16)
    rows_ref[...] = rows
    copies_ref[...] = jnp.broadcast_to(rows[None], copies_ref.shape)


def spread(parts, copies):
    count = sum(part.shape[0] for part in parts)
    width = parts[0].shape[1]
    return pl.pallas_call(
        spread_kernel,
        out_shape=[
            jax.ShapeDtypeStruct((count, width), BF16),
            jax.ShapeDtypeStruct((copies, count, width), BF16),
        ],
        compiler_params=pltpu.CompilerParams(vmem_limit_bytes=8 * 2**20),
    )(*parts)


def split_pair(values):
    high = values.astype(BF16)
    return high, (values - high.astype(F32)).astype(BF16)


def pair_slope(logits, same):
    signs = jnp.where(same, 1.0, -1.0).astype(F32)
    return -signs * jax.nn.sigmoid(-signs * logits)


def weighted_sum(coeff, rows):
    high, low = split_pair(coeff)
    both = jnp.dot(jnp.concatenate([high, low], axis=0), rows, preferred_element_type=F32)
    count = coeff.shape[0]
    return SIMILARITY_HEAT * (both[:count] + both[count:])


def held(*values):
    return lax.optimization_barrier(values)


def moved(values, target, mesh_shape):
    wide, deep, cores = mesh_shape
    pairs = []
    for index in range(wide * deep * cores):
        y, z, core = index // (deep * cores), index // cores % deep, index % cores
        y, z, core = target(y, z, core)
        pairs.append((index, (y % wide * deep + z % deep) * cores + core % cores))
    return lax.ppermute(values, "expert", pairs)


def along_expert(copies, shape):
    wide, deep, cores = shape
    chips = wide * deep
    groups = [[chip * cores + core for chip in range(chips)] for core in range(cores)]
    column = lax.all_to_all(
        copies, "expert", split_axis=0, concat_axis=0, axis_index_groups=groups, tiled=True
    ).reshape(chips * copies.shape[1], copies.shape[2])
    return on_chip(column, shape)


def on_chip(group, shape):
    return jnp.concatenate([group, moved(group, lambda y, z, c: (y, z, c + 1), shape)], axis=0)


def ring_shift(values, step, size):
    return lax.ppermute(values, "grid", [(i, (i + step) % size) for i in range(size)])


def unit_rows(values):
    return values * lax.rsqrt(jnp.mean(values * values, axis=-1, keepdims=True) + EPSILON)


def on_device(
    tokens, routes, route_gates, caption_lengths, image_embed, final_gain, up_weight, down_weight
):
    token_count, width = tokens.shape
    experts_all = lax.axis_size("expert")
    grid_all = lax.axis_size("grid")
    slots = 4 * token_count // experts_all
    places_all = experts_all * slots
    scale_root = math.sqrt(width)

    picture_unit = (unit_rows(image_embed.astype(F32)) / scale_root).astype(BF16)
    captions_here = picture_unit.shape[0]
    shape = (grid_all, experts_all // (2 * grid_all), 2)
    chip = lax.axis_index("expert") // shape[2]

    row_parts = [picture_unit] + [ring_shift(picture_unit, k, grid_all) for k in range(1, grid_all)]
    send, place = dispatch(tokens, routes.T, places_all, slots)
    send = send.reshape(experts_all, slots, width)
    arrived = lax.all_to_all(send, "expert", split_axis=0, concat_axis=0, tiled=True)
    chips = shape[0] * shape[1]
    pictures_row, picture_copies = spread(row_parts, chips)
    arrived, picture_copies, pictures_row = held(arrived, picture_copies, pictures_row)
    rows = arrived.reshape(places_all, width)

    up_local = up_weight[0]
    down_local = down_weight[0]
    half = places_all // 2
    top, bottom = rows[:half], rows[half:]
    left_top = ring_shift(top, 1, grid_all)
    right_bottom = ring_shift(bottom, -1, grid_all)
    pictures_all = along_expert(picture_copies, shape)
    left_bottom = ring_shift(bottom, 1, grid_all)
    right_top = ring_shift(top, -1, grid_all)
    own_term = expert_part([rows], up_local, down_local)[0]
    own_term, left_top, right_bottom = held(own_term, left_top, right_bottom)
    far_top = ring_shift(left_top, 1, grid_all)
    far_bottom = ring_shift(right_bottom, -1, grid_all)
    left_top, right_bottom = expert_part([left_top, right_bottom], up_local, down_local)
    home_top = ring_shift(left_top, -1, grid_all)
    home_bottom = ring_shift(right_bottom, 1, grid_all)
    right_top, left_bottom, left_top, right_bottom = held(
        right_top, left_bottom, left_top, right_bottom
    )
    right_top, left_bottom = expert_part([right_top, left_bottom], up_local, down_local)
    far_top, far_bottom, left_top, right_bottom, right_top, left_bottom = held(
        far_top, far_bottom, left_top, right_bottom, right_top, left_bottom
    )
    far_top, far_bottom = expert_part([far_top, far_bottom], up_local, down_local)
    far_from_left = ring_shift(far_top, 1, grid_all)
    far_from_right = ring_shift(far_bottom, -1, grid_all)
    far_from_left, far_from_right, home_top, home_bottom = held(
        far_from_left, far_from_right, home_top, home_bottom
    )
    right_top = (right_top.astype(F32) + far_from_left.astype(F32)).astype(BF16)
    left_bottom = (left_bottom.astype(F32) + far_from_right.astype(F32)).astype(BF16)
    last_top = ring_shift(right_top, 1, grid_all)
    last_bottom = ring_shift(left_bottom, -1, grid_all)
    total = sum_terms(own_term, home_top, last_top, home_bottom, last_bottom)
    results = total.reshape(experts_all, slots, width)
    returned = lax.all_to_all(results, "expert", split_axis=0, concat_axis=0, tiled=True)
    returned, pictures_all = held(returned, pictures_all)
    returned = returned.reshape(places_all, width)

    text_embed, text_copies = combine(
        caption_lengths, returned, tokens, place, route_gates.T, final_gain, chips
    )
    text_unit = text_copies[0]
    text_column = along_expert(text_copies, shape)

    def slopes(mine, others, place):
        logits = SIMILARITY_HEAT * lax.dot_general(
            mine, others, (((1,), (1,)), ((), ())), preferred_element_type=F32
        )
        row_ids = lax.broadcasted_iota(jnp.int32, logits.shape, 0)
        column_ids = lax.broadcasted_iota(jnp.int32, logits.shape, 1)
        same = (row_ids < captions_here) & (row_ids + place == column_ids)
        return weighted_sum(pair_slope(logits, same), others)

    sentence_slope = slopes(text_unit, pictures_all, chip * pictures_row.shape[0])
    partial = slopes(pictures_row, text_column, chip * captions_here).reshape(grid_all, captions_here, width)
    picture_slope = partial[0]
    for k in range(1, grid_all):
        picture_slope = picture_slope + ring_shift(partial[k], -k, grid_all)
    return (text_embed, sentence_slope, picture_slope)


def solution(mesh):
    split = P(("expert", "grid"), None)
    weights = P("expert", None, "grid")

    return jax.shard_map(
        on_device,
        mesh=mesh,
        in_specs=(split, split, split, split, split, P(), weights, weights),
        out_specs=(split, split, split),
        check_vma=False,
    )
```

```python
import functools
import math

import jax
import jax.numpy as jnp
from jax import lax
from jax.experimental import pallas as pl
from jax.experimental.pallas import tpu as pltpu
from jax.sharding import PartitionSpec as P

EPSILON = 1e-06
SIMILARITY_HEAT = 10.0
BF16 = jnp.bfloat16
F32 = jnp.float32


def layer_norm(values):
    centred = values - jnp.mean(values, axis=-1, keepdims=True)
    return centred * lax.rsqrt(jnp.mean(centred * centred, axis=-1, keepdims=True) + EPSILON)


def expert_kernel(*refs):
    blocks = (len(refs) - 3) // 2
    rows_refs, (up_ref, down_ref) = refs[:blocks], refs[blocks : blocks + 2]
    out_refs, hidden_ref = refs[blocks + 2 : -1], refs[-1]
    step = pl.program_id(0)
    half = pl.num_programs(0) // 2
    tile = up_ref.shape[1]

    @pl.when(step < half)
    def _():
        rows = jnp.concatenate([ref[...] for ref in rows_refs], axis=0)
        hidden = jnp.dot(rows, up_ref[...], preferred_element_type=F32)
        hidden = (0.5 * hidden * (1.0 + lax.erf(hidden * math.sqrt(0.5)))).astype(BF16)
        hidden_ref[:, pl.ds(pl.multiple_of(step * tile, tile), tile)] = hidden

    @pl.when(step >= half)
    def _():
        term = lax.dot_general(
            hidden_ref[...], down_ref[...], (((1,), (1,)), ((), ())), preferred_element_type=F32
        ).astype(BF16)
        start = 0
        for ref in out_refs:
            ref[...] = term[start : start + ref.shape[0]]
            start += ref.shape[0]


def expert_part(blocks, up_piece, down_piece):
    width, units = up_piece.shape
    count = sum(block.shape[0] for block in blocks)
    tile = min(512, units)
    half = units // tile
    return pl.pallas_call(
        expert_kernel,
        grid=(2 * half,),
        in_specs=[pl.BlockSpec(block.shape, lambda i: (0, 0)) for block in blocks]
        + [
            pl.BlockSpec((width, tile), lambda i: (0, jnp.minimum(i, half - 1))),
            pl.BlockSpec((width // half, units), lambda i: (jnp.maximum(i - half, 0), 0)),
        ],
        out_specs=[
            pl.BlockSpec((block.shape[0], width // half), lambda i: (0, jnp.maximum(i - half, 0)))
            for block in blocks
        ],
        out_shape=[jax.ShapeDtypeStruct(block.shape, BF16) for block in blocks],
        scratch_shapes=[pltpu.VMEM((count, units), BF16)],
        compiler_params=pltpu.CompilerParams(vmem_limit_bytes=56 * 2**20),
        cost_estimate=pl.CostEstimate(
            flops=12 * count * width * units,
            bytes_accessed=4 * width * units + 4 * count * width,
            transcendentals=count * units,
        ),
    )(*blocks, up_piece, down_piece)


def sum_kernel(own_ref, home_top, last_top, home_bottom, last_bottom, out_ref):
    own = own_ref[...].astype(F32)
    early = pl.program_id(0) < pl.num_programs(0) // 2

    @pl.when(early)
    def _():
        out_ref[...] = (own + home_top[...].astype(F32) + last_top[...].astype(F32)).astype(BF16)

    @pl.when(jnp.logical_not(early))
    def _():
        out_ref[...] = (
            own + home_bottom[...].astype(F32) + last_bottom[...].astype(F32)
        ).astype(BF16)


def sum_terms(own, home_top, last_top, home_bottom, last_bottom):
    count, width = own.shape
    steps = 2
    block = (count // steps, width)
    top = pl.BlockSpec(block, lambda i: (jnp.minimum(i, steps // 2 - 1), 0))
    bottom = pl.BlockSpec(block, lambda i: (jnp.maximum(i - steps // 2, 0), 0))
    return pl.pallas_call(
        sum_kernel,
        grid=(steps,),
        in_specs=[pl.BlockSpec(block, lambda i: (i, 0)), top, top, bottom, bottom],
        out_specs=pl.BlockSpec(block, lambda i: (i, 0)),
        out_shape=jax.ShapeDtypeStruct(own.shape, BF16),
        compiler_params=pltpu.CompilerParams(vmem_limit_bytes=16 * 2**20),
    )(own, home_top, last_top, home_bottom, last_bottom)


def dispatch_kernel(slots, tokens_ref, routes_ref, send_ref, place_ref, normed_ref):
    count = tokens_ref.shape[0]
    rows = send_ref.shape[0]
    step = pl.program_id(0)

    @pl.when(step == 0)
    def _():
        normed_ref[...] = layer_norm(tokens_ref[...].astype(F32)).astype(BF16)
        first, second = routes_ref[0:1, :], routes_ref[1:2, :]
        experts = rows * pl.num_programs(0) // slots
        names = lax.broadcasted_iota(jnp.int32, (experts, count), 0)
        hot_first = (first == names).astype(F32)
        hot_second = (second == names).astype(F32)
        column_ids = lax.broadcasted_iota(jnp.int32, (count, count), 1)
        row_ids = lax.broadcasted_iota(jnp.int32, (count, count), 0)
        before = (row_ids < column_ids).astype(F32).astype(BF16)
        rank_first = jnp.dot(hot_first.astype(BF16), before, preferred_element_type=F32)
        rank_second = jnp.dot(hot_second.astype(BF16), before, preferred_element_type=F32)
        rank_second = rank_second + jnp.sum(hot_first, axis=1, keepdims=True)
        rank_first = jnp.sum(rank_first * hot_first, axis=0, keepdims=True)
        rank_second = jnp.sum(rank_second * hot_second, axis=0, keepdims=True)
        place_ref[0:1, :] = first * slots + rank_first.astype(jnp.int32)
        place_ref[1:2, :] = second * slots + rank_second.astype(jnp.int32)

    spots = lax.broadcasted_iota(jnp.int32, (rows, count), 0) + step * rows
    chosen = ((spots == place_ref[0:1, :]) | (spots == place_ref[1:2, :])).astype(F32)
    send = jnp.dot(chosen.astype(BF16), normed_ref[...], preferred_element_type=F32)
    send_ref[...] = send.astype(BF16)


def dispatch(tokens, routes, places, slots):
    steps = 4
    count, width = tokens.shape
    return pl.pallas_call(
        functools.partial(dispatch_kernel, slots),
        grid=(steps,),
        in_specs=[
            pl.BlockSpec(tokens.shape, lambda i: (0, 0)),
            pl.BlockSpec(routes.shape, lambda i: (0, 0)),
        ],
        out_specs=[
            pl.BlockSpec((places // steps, width), lambda i: (i, 0)),
            pl.BlockSpec(routes.shape, lambda i: (0, 0)),
        ],
        out_shape=[
            jax.ShapeDtypeStruct((places, width), BF16),
            jax.ShapeDtypeStruct(routes.shape, jnp.int32),
        ],
        scratch_shapes=[pltpu.VMEM((count, width), BF16)],
        compiler_params=pltpu.CompilerParams(vmem_limit_bytes=63 * 2**20),
    )(tokens, routes)


def combine_kernel(
    lengths_ref, returned_ref, tokens_ref, place_ref, gates_ref, gain_ref, embed_ref, copies_ref
):
    count = tokens_ref.shape[0]
    captions = embed_ref.shape[0]
    returned = returned_ref[...]
    spots = lax.broadcasted_iota(jnp.int32, (count, returned.shape[0]), 1)
    zeros = jnp.zeros((4, count), F32)
    columns = jnp.concatenate([place_ref[...].astype(F32), gates_ref[...], zeros], axis=0).T
    places = columns[:, 0:2].astype(jnp.int32)
    gates = jnp.where(spots == places[:, 0:1], columns[:, 2:3], 0.0) + jnp.where(
        spots == places[:, 1:2], columns[:, 3:4], 0.0
    )
    high, low = split_pair(gates)
    both = jnp.dot(
        jnp.concatenate([high, low], axis=0), returned, preferred_element_type=F32
    )
    mixed = tokens_ref[...].astype(F32) + both[:count] + both[count:]
    final = layer_norm(mixed) * gain_ref[...]
    padded = 8
    caption = lax.broadcasted_iota(jnp.int32, (padded, count), 0)
    token = lax.broadcasted_iota(jnp.int32, (padded, count), 1)
    row = lax.broadcasted_iota(jnp.int32, (padded, 1), 0)
    inside = jnp.zeros((padded, count), F32)
    sizes = jnp.ones((padded, 1), F32)
    start = jnp.int32(0)
    for index in range(captions):
        size = lengths_ref[0, index]
        here = (caption == index) & (token >= start) & (token < start + size)
        inside = jnp.where(here, 1.0, inside)
        sizes = jnp.where(row == index, size.astype(F32), sizes)
        start = start + size
    inside = inside.astype(BF16)
    first, rest = final.astype(BF16), final
    pooled = jnp.dot(inside, first, preferred_element_type=F32)
    for _ in range(2):
        rest = rest - first.astype(F32)
        first = rest.astype(BF16)
        pooled += jnp.dot(inside, first, preferred_element_type=F32)
    embed = unit_rows(pooled / sizes)[:captions]
    embed_ref[...] = embed
    unit = (embed * (1.0 / math.sqrt(embed.shape[1]))).astype(BF16)
    copies_ref[...] = jnp.broadcast_to(unit[None], copies_ref.shape)


def combine(lengths, returned, tokens, place, gates, gain, copies):
    captions = lengths.shape[1]
    width = tokens.shape[1]
    vmem = pl.BlockSpec(memory_space=pltpu.VMEM)
    return pl.pallas_call(
        combine_kernel,
        in_specs=[pl.BlockSpec(memory_space=pltpu.SMEM)] + [vmem] * 5,
        out_specs=[vmem, vmem],
        out_shape=[
            jax.ShapeDtypeStruct((captions, width), F32),
            jax.ShapeDtypeStruct((copies, captions, width), BF16),
        ],
        compiler_params=pltpu.CompilerParams(vmem_limit_bytes=24 * 2**20),
    )(lengths, returned, tokens, place, gates, gain.reshape(1, width))


def spread_kernel(*refs):
    rows_ref, copies_ref = refs[-2:]
    rows = jnp.concatenate([ref[...].astype(F32) for ref in refs[:-2]], axis=0).astype(BF16)
    rows_ref[...] = rows
    copies_ref[...] = jnp.broadcast_to(rows[None], copies_ref.shape)


def spread(parts, copies):
    count = sum(part.shape[0] for part in parts)
    width = parts[0].shape[1]
    return pl.pallas_call(
        spread_kernel,
        out_shape=[
            jax.ShapeDtypeStruct((count, width), BF16),
            jax.ShapeDtypeStruct((copies, count, width), BF16),
        ],
        compiler_params=pltpu.CompilerParams(vmem_limit_bytes=8 * 2**20),
    )(*parts)


def split_pair(values):
    high = values.astype(BF16)
    return high, (values - high.astype(F32)).astype(BF16)


def pair_slope(logits, same):
    signs = jnp.where(same, 1.0, -1.0).astype(F32)
    return -signs * jax.nn.sigmoid(-signs * logits)


def weighted_sum(coeff, rows):
    high, low = split_pair(coeff)
    both = jnp.dot(jnp.concatenate([high, low], axis=0), rows, preferred_element_type=F32)
    count = coeff.shape[0]
    return SIMILARITY_HEAT * (both[:count] + both[count:])


def held(*values):
    return lax.optimization_barrier(values)


def moved(values, target, mesh_shape):
    wide, deep, cores = mesh_shape
    pairs = []
    for index in range(wide * deep * cores):
        y, z, core = index // (deep * cores), index // cores % deep, index % cores
        y, z, core = target(y, z, core)
        pairs.append((index, (y % wide * deep + z % deep) * cores + core % cores))
    return lax.ppermute(values, "expert", pairs)


def along_expert(copies, shape):
    wide, deep, cores = shape
    chips = wide * deep
    groups = [[chip * cores + core for chip in range(chips)] for core in range(cores)]
    column = lax.all_to_all(
        copies, "expert", split_axis=0, concat_axis=0, axis_index_groups=groups, tiled=True
    ).reshape(chips * copies.shape[1], copies.shape[2])
    return on_chip(column, shape)


def on_chip(group, shape):
    return jnp.concatenate([group, moved(group, lambda y, z, c: (y, z, c + 1), shape)], axis=0)


def ring_shift(values, step, size):
    return lax.ppermute(values, "grid", [(i, (i + step) % size) for i in range(size)])


def unit_rows(values):
    return values * lax.rsqrt(jnp.mean(values * values, axis=-1, keepdims=True) + EPSILON)


def on_device(
    tokens, routes, route_gates, caption_lengths, image_embed, final_gain, up_weight, down_weight
):
    token_count, width = tokens.shape
    experts_all = lax.axis_size("expert")
    grid_all = lax.axis_size("grid")
    slots = 4 * token_count // experts_all
    places_all = experts_all * slots
    scale_root = math.sqrt(width)

    picture_unit = (unit_rows(image_embed.astype(F32)) / scale_root).astype(BF16)
    captions_here = picture_unit.shape[0]
    shape = (grid_all, experts_all // (2 * grid_all), 2)
    chip = lax.axis_index("expert") // shape[2]

    row_parts = [picture_unit] + [ring_shift(picture_unit, k, grid_all) for k in range(1, grid_all)]
    send, place = dispatch(tokens, routes.T, places_all, slots)
    send = send.reshape(experts_all, slots, width)
    arrived = lax.all_to_all(send, "expert", split_axis=0, concat_axis=0, tiled=True)
    chips = shape[0] * shape[1]
    pictures_row, picture_copies = spread(row_parts, chips)
    arrived, picture_copies, pictures_row = held(arrived, picture_copies, pictures_row)
    rows = arrived.reshape(places_all, width)

    up_local = up_weight[0]
    down_local = down_weight[0]
    half = places_all // 2
    top, bottom = rows[:half], rows[half:]
    left_top = ring_shift(top, 1, grid_all)
    right_bottom = ring_shift(bottom, -1, grid_all)
    pictures_all = along_expert(picture_copies, shape)
    left_bottom = ring_shift(bottom, 1, grid_all)
    right_top = ring_shift(top, -1, grid_all)
    own_term = expert_part([rows], up_local, down_local)[0]
    own_term, left_top, right_bottom = held(own_term, left_top, right_bottom)
    far_top = ring_shift(left_top, 1, grid_all)
    far_bottom = ring_shift(right_bottom, -1, grid_all)
    left_top, right_bottom = expert_part([left_top, right_bottom], up_local, down_local)
    home_top = ring_shift(left_top, -1, grid_all)
    home_bottom = ring_shift(right_bottom, 1, grid_all)
    right_top, left_bottom, left_top, right_bottom = held(
        right_top, left_bottom, left_top, right_bottom
    )
    right_top, left_bottom = expert_part([right_top, left_bottom], up_local, down_local)
    far_top, far_bottom, left_top, right_bottom, right_top, left_bottom = held(
        far_top, far_bottom, left_top, right_bottom, right_top, left_bottom
    )
    far_top, far_bottom = expert_part([far_top, far_bottom], up_local, down_local)
    far_from_left = ring_shift(far_top, 1, grid_all)
    far_from_right = ring_shift(far_bottom, -1, grid_all)
    far_from_left, far_from_right, home_top, home_bottom = held(
        far_from_left, far_from_right, home_top, home_bottom
    )
    right_top = (right_top.astype(F32) + far_from_left.astype(F32)).astype(BF16)
    left_bottom = (left_bottom.astype(F32) + far_from_right.astype(F32)).astype(BF16)
    last_top = ring_shift(right_top, 1, grid_all)
    last_bottom = ring_shift(left_bottom, -1, grid_all)
    total = sum_terms(own_term, home_top, last_top, home_bottom, last_bottom)
    results = total.reshape(experts_all, slots, width)
    returned = lax.all_to_all(results, "expert", split_axis=0, concat_axis=0, tiled=True)
    returned, pictures_all = held(returned, pictures_all)
    returned = returned.reshape(places_all, width)

    text_embed, text_copies = combine(
        caption_lengths, returned, tokens, place, route_gates.T, final_gain, chips
    )
    text_unit = text_copies[0]
    text_column = along_expert(text_copies, shape)

    def slopes(mine, others, place):
        logits = SIMILARITY_HEAT * lax.dot_general(
            mine, others, (((1,), (1,)), ((), ())), preferred_element_type=F32
        )
        row_ids = lax.broadcasted_iota(jnp.int32, logits.shape, 0)
        column_ids = lax.broadcasted_iota(jnp.int32, logits.shape, 1)
        same = (row_ids < captions_here) & (row_ids + place == column_ids)
        return weighted_sum(pair_slope(logits, same), others)

    sentence_slope = slopes(text_unit, pictures_all, chip * pictures_row.shape[0])
    partial = slopes(pictures_row, text_column, chip * captions_here).reshape(grid_all, captions_here, width)
    picture_slope = partial[0]
    for k in range(1, grid_all):
        picture_slope = picture_slope + ring_shift(partial[k], -k, grid_all)
    return (text_embed, sentence_slope, picture_slope)


def solution(mesh):
    split = P(("expert", "grid"), None)
    weights = P("expert", None, "grid")

    return jax.shard_map(
        on_device,
        mesh=mesh,
        in_specs=(split, split, split, split, split, P(), weights, weights),
        out_specs=(split, split, split),
        check_vma=False,
    )
```
